256 devices in a mesh: depth: 8 (over x, z_lo), sky: 32 (over y, z_hi, core).
Axes of the slice: x: 4, y: 4, z: 8 (z_hi: 4, z_lo: 2; z = z_hi * 2 + z_lo), core: 2. Of those that a mesh axis runs over, the one named last changes fastest.
Arguments:
- potential: float32 [96, 1024, 2048], P('depth', 'sky'), may hold values from -6 to 6
- widths: int32 [96], P('depth'), may hold values from 1 to 8, as said below
- plane_slot: int32 [96], P('depth'), may hold values from 0 to 15
- ratio_near: float32 [16], replicated, may hold values from 1 to 1.6
- ratio_lens: float32 [16], replicated, may hold values from 0.5 to 1.5
Outputs:
- convergence: float32 [96, 1024, 2048], P('depth', 'sky')
The draws below stay inside these ranges and needn't reach their ends.
Inputs may be any that keep to these rules, and one draw needn't show every extreme that they name: `widths`: some plane has half-width 8.
All inputs are finite; a program needn't handle non-finite values.
Results may differ from the reference program's by a relative error of at most 0.0003.
Values sent between devices are 32-bit elements; how exact they have to be, the bound alone decides.
A program may use at most 64 MiB of HBM per device.

```python
import jax
import jax.numpy as jnp
from jax import lax

PL_DEV = 12
COLS = 2048
WMAX = 8
TABLE = 16
PLANES = 96
ROWS = 1024


def draw_widths(key, part):
    first_key = jax.random.fold_in(key, 11)
    second_key = jax.random.fold_in(key, 23)
    base_widths = jax.random.randint(first_key, (PLANES,), 1, WMAX + 1)
    block_count = PLANES // PL_DEV
    position = jax.random.randint(second_key, (block_count,), 0, PL_DEV)
    lanes = jnp.arange(PLANES, dtype=jnp.int32) % PL_DEV
    blocks = jnp.arange(PLANES, dtype=jnp.int32) // PL_DEV
    return jnp.where(lanes == position[blocks], WMAX, base_widths).astype(jnp.int32)


def place_ends(entries, own_key, least, top_value):
    spot = [jax.random.randint(jax.random.fold_in(own_key, axis), (), 0, length) for axis, length in enumerate(entries.shape)]
    main_axis = entries.shape.index(max(entries.shape))
    next_to = spot[:main_axis] + [(spot[main_axis] + 1) % entries.shape[main_axis]] + spot[main_axis + 1:]
    return entries.at[tuple(spot)].set(least).at[tuple(next_to)].set(top_value)


def levels(own_key, dims, shards, low, high):
    factor_of, own = 1.0, jax.random.fold_in(own_key, 6)
    for dim, parts in shards:
        draws = jnp.exp(jax.random.uniform(jax.random.fold_in(own, dim), (parts,), jnp.float32, low / len(shards), high / len(shards)))
        factor_of = factor_of * jnp.repeat(draws, dims[dim] // parts).reshape([-1 if axis == dim else 1 for axis in range(len(dims))])
    return factor_of


def bell_draw(own_key, shape, scale, most, pieces=(), kind=jnp.bfloat16):
    values = scale * jax.random.normal(own_key, shape, jnp.float32)
    if pieces:
        values = values * levels(own_key, shape, pieces, -0.22, 0.18)
    return jnp.clip(values, -most, most).astype(kind)


def setup_inputs(seed: int = 0) -> dict:
    keys = jax.random.split(jax.random.key(seed), 6)
    return {
        "potential": bell_draw(keys[0], (PLANES, ROWS, COLS), 0.5, 6.0, ((0, 8), (1, 32)), jnp.float32),
        "widths": draw_widths(jax.random.fold_in(keys[5], 71), 0),
        "plane_slot": place_ends(jax.random.randint(keys[2], (PLANES,), 0, TABLE), jax.random.fold_in(keys[2], 1), 0, TABLE - 1).astype(jnp.int32),
        "ratio_near": jnp.clip(jax.random.uniform(keys[3], (TABLE,), jnp.float32, 1.0, 1.6), 1.0, 1.6),
        "ratio_lens": jnp.clip(jax.random.uniform(keys[4], (TABLE,), jnp.float32, 0.5, 1.5), 0.5, 1.5),
    }


def box_filter(values, half_width, axis_index, length):
    summed = None
    for displace in range(-WMAX, WMAX + 1):
        window = lax.slice_in_dim(values, WMAX + displace, WMAX + displace + length, axis=axis_index)
        active = jnp.where(abs(displace) <= half_width, 1.0, 0.0).astype(jnp.float32)
        term = active * window
        summed = term if summed is None else summed + term
    return summed / (2.0 * half_width.astype(jnp.float32) + 1.0)


def hessian(padded, half_width, row_count, col_count):
    along = box_filter(padded, half_width, 0, row_count + 2)
    smooth = box_filter(along, half_width, 1, col_count + 2)
    centre = smooth[1:-1, 1:-1]
    along_cols = smooth[1:-1, 2:] - 2.0 * centre + smooth[1:-1, :-2]
    along_rows = smooth[2:, 1:-1] - 2.0 * centre + smooth[:-2, 1:-1]
    mixed_term = 0.25 * (smooth[2:, 2:] - smooth[2:, :-2] - smooth[:-2, 2:] + smooth[:-2, :-2])
    return along_cols, along_rows, mixed_term


def advance(carried, along_cols, along_rows, mixed_term, near_factor, lens_factor):
    entry_xx = near_factor - lens_factor * along_cols
    entry_yy = near_factor - lens_factor * along_rows
    entry_xy = -lens_factor * mixed_term
    retained = 1.0 - near_factor
    upper = carried[0:2]
    lower = carried[2:4]
    row_first = entry_xx * upper[0] + entry_xy * upper[1] + retained * lower[0]
    row_second = entry_xy * upper[0] + entry_yy * upper[1] + retained * lower[1]
    advanced = jnp.stack([row_first, row_second, upper[0], upper[1]])
    convergence = 1.0 - 0.5 * (row_first[0] + row_second[1])
    return advanced, convergence


def identity_state(row_count, col_count):
    pattern = jnp.array([[1.0, 0.0], [0.0, 1.0], [1.0, 0.0], [0.0, 1.0]], dtype=jnp.float32)
    return jnp.broadcast_to(pattern[:, :, None, None], (4, 2, row_count, col_count)).astype(jnp.float32)


def reference(potential, widths, plane_slot, ratio_near, ratio_lens):
    row_count = potential.shape[1]
    col_count = potential.shape[2]
    table_ids = jnp.arange(ratio_near.shape[0], dtype=jnp.int32)

    def plane(carried, inputs):
        plane_map, half_width, slot_id = inputs
        chosen = (slot_id == table_ids).astype(jnp.float32)
        near_factor = jnp.sum(chosen * ratio_near)
        lens_factor = jnp.sum(chosen * ratio_lens)
        padded = jnp.pad(plane_map, WMAX + 1)
        along_cols, along_rows, mixed_term = hessian(padded, half_width, row_count, col_count)
        return advance(carried, along_cols, along_rows, mixed_term, near_factor, lens_factor)

    initial = identity_state(row_count, col_count)
    final_state, convergence = lax.scan(plane, initial, (potential, widths, plane_slot))
    return convergence
```

```python
import jax
import jax.numpy as jnp
from jax import lax
from jax.experimental import pallas as pl
from jax.experimental.pallas import tpu as pltpu
from jax.sharding import PartitionSpec as P

WMAX = 8
LANES = 128
EIGHT = 8
TILE = 256
FAR = 1000
MESH = pl.DeviceIdType.MESH
F32 = jnp.float32
BF16 = jnp.bfloat16


def round_up(value, step):
    return -(-value // step) * step


def split(values):
    high = values.astype(BF16)
    return high, (values - high.astype(F32)).astype(BF16)


def stencils(distance, half_width):
    inside = lambda shift: jnp.where(jnp.abs(distance + shift) <= half_width, 1.0, 0.0)
    after, here, before = inside(-1), inside(0), inside(1)
    return here.astype(BF16), (after - 2.0 * here + before).astype(BF16), (after - before).astype(BF16)


def kernel(
    width_ref, slot_ref, near_ref, lens_ref, pot_ref, out_ref,
    own, top, bot, pack, rowm, colm, coef, arrived, leaving, conv,
    load_sem, halo_send, halo_recv, state_send, state_recv, store_sem,
):
    depth, sky = lax.axis_index("depth"), lax.axis_index("sky")
    has_before, has_after = sky > 0, sky < lax.axis_size("sky") - 1
    takes, gives = depth > 0, depth < lax.axis_size("depth") - 1
    planes, rows, cols = pot_ref.shape
    ninth = pack.shape[1]
    pieces, tiles, bands = cols // LANES, cols // TILE, rows // EIGHT
    middle = pl.ds(LANES, cols)

    load = pltpu.make_async_copy(pot_ref, own.at[:, :, middle], load_sem)
    load.start()
    barrier = pltpu.get_barrier_semaphore()
    partners = (
        (has_before, {"sky": sky - 1}), (has_after, {"sky": sky + 1}),
        (takes, {"depth": depth - 1}), (gives, {"depth": depth + 1}),
    )
    for there, partner in partners:
        @pl.when(there)
        def _(partner=partner):
            pl.semaphore_signal(barrier, inc=1, device_id=partner, device_id_type=MESH)

    for buffer in (own, top, bot):
        for edge in (pl.ds(0, LANES), pl.ds(LANES + cols, LANES)):
            buffer[:, :, edge] = jnp.zeros((buffer.shape[0], buffer.shape[1], LANES), F32)
    for there, buffer in ((has_before, top), (has_after, bot)):
        @pl.when(jnp.logical_not(there))
        def _(buffer=buffer):
            buffer[...] = jnp.zeros_like(buffer)
    pack[...] = jnp.zeros_like(pack)
    load.wait()
    for side, row in ((0, rows - WMAX - 1), (1, WMAX)):
        for k in range(planes):
            pack[side, k // EIGHT, pl.ds(k % EIGHT, 1), :] = own[k, pl.ds(row, 1), middle]

    pl.semaphore_wait(barrier, sum(there.astype(jnp.int32) for there, _ in partners))

    def halo(side, part, piece):
        col = pl.multiple_of(piece * LANES, LANES)
        landing = (top, bot)[side]
        lanes_there = pl.ds(pl.multiple_of(col + LANES, LANES), LANES)
        if part == 0:
            source = pot_ref.at[:, pl.ds((rows - WMAX, 0)[side], WMAX), pl.ds(col, LANES)]
            target = landing.at[pl.ds(0, planes), :, lanes_there]
        else:
            source = pack.at[side, :, :, pl.ds(col, LANES)]
            target = landing.at[pl.ds(planes, ninth), :, lanes_there]
        return pltpu.make_async_remote_copy(
            src_ref=source, dst_ref=target,
            send_sem=halo_send.at[side, part, piece], recv_sem=halo_recv.at[side, part, piece],
            device_id={"sky": sky + (1, -1)[side]}, device_id_type=MESH,
        )

    sends, lands = (has_after, has_before), (has_before, has_after)

    def send_halo(piece, carry):
        for side in (0, 1):
            @pl.when(sends[side])
            def _(side=side):
                halo(side, 0, piece).start()
                halo(side, 1, piece).start()
        return carry

    lax.fori_loop(0, pieces, send_halo, 0)

    def await_halo(piece):
        for side in (0, 1):
            @pl.when(lands[side])
            def _(side=side):
                halo(side, 0, piece).wait_recv()
                halo(side, 1, piece).wait_recv()

    @pl.when(jnp.logical_not(takes))
    def _():
        def start(tile, carry):
            for entry in range(8):
                arrived[tile, entry] = jnp.full((EIGHT, TILE), (1.0, 0.0, 0.0, 1.0)[entry % 4], F32)
            return carry
        lax.fori_loop(0, tiles * bands, start, 0)

    own_rows = rows + 2 * WMAX
    tall = own_rows + 2 * EIGHT * ninth

    def build(k, carry):
        half_width = width_ref[k]
        place = lax.broadcasted_iota(jnp.int32, (rows, 2 * tall), 1)
        place = jnp.where(place >= tall, place - tall, place)
        far_up = jnp.where(place - own_rows == k, -WMAX - 1, FAR)
        far_down = jnp.where(place - own_rows - EIGHT * ninth == k, rows + WMAX, FAR)
        row = jnp.where(place < rows, place, jnp.where(
            place < rows + WMAX, place - rows - WMAX, jnp.where(
                place < own_rows, place - WMAX, jnp.where(
                    place < own_rows + EIGHT * ninth, far_up, far_down))))
        box, second, central = stencils(row - lax.broadcasted_iota(jnp.int32, (rows, 2 * tall), 0), half_width)
        rowm[k, 0:rows, :] = box
        rowm[k, rows:2 * rows, :] = second
        rowm[k, 2 * rows:3 * rows, :] = central
        shape = (3 * LANES, LANES)
        gap = lax.broadcasted_iota(jnp.int32, shape, 0) - lax.broadcasted_iota(jnp.int32, shape, 1) - LANES
        box, second, central = stencils(gap, half_width)
        colm[k, 0] = second
        colm[k, 1] = box
        colm[k, 2] = central
        return carry

    lax.fori_loop(0, planes, build, 0)

    def curvature(tile):
        col = pl.multiple_of(tile * TILE, TILE)
        window = pl.ds(col, TILE + 2 * LANES)

        def plane(k, carry):
            half_width = width_ref[k]
            near = near_ref[slot_ref[k]]
            lens = lens_ref[slot_ref[k]]
            share = jnp.float32(1.0 / (2 * WMAX + 1) ** 2)
            for width in range(1, WMAX):
                share = jnp.where(half_width == width, jnp.float32(1.0 / (2 * width + 1) ** 2), share)
            strength = lens * share
            values = [own[k, :, window], top[k, :, window], bot[k, :, window]]
            values += [buffer[planes + i, :, window] for buffer in (top, bot) for i in range(ninth)]
            tall_values = jnp.concatenate(split(jnp.concatenate(values, axis=0)), axis=0)
            along = jnp.dot(rowm[k], tall_values, preferred_element_type=F32)
            along_high, along_low = split(along)
            for kind in range(3):
                band = slice(kind * rows, (kind + 1) * rows)
                left, right = slice(0, 3 * LANES), slice(LANES, 4 * LANES)
                stacked = jnp.concatenate([
                    along_high[band, left], along_low[band, left],
                    along_high[band, right], along_low[band, right]], axis=0)
                both = jnp.dot(stacked, colm[k, kind], preferred_element_type=F32)
                full = jnp.concatenate([
                    both[0:rows] + both[rows:2 * rows],
                    both[2 * rows:3 * rows] + both[3 * rows:4 * rows]], axis=1)
                if kind == 2:
                    coef[k, kind, :, pl.ds(col, TILE)] = (-0.25 * strength) * full
                else:
                    coef[k, kind, :, pl.ds(col, TILE)] = near - strength * full
            return carry

        lax.fori_loop(0, planes, plane, 0)

    def state(index):
        return pltpu.make_async_remote_copy(
            src_ref=leaving.at[index], dst_ref=arrived.at[index],
            send_sem=state_send.at[index], recv_sem=state_recv.at[index],
            device_id={"depth": depth + 1}, device_id_type=MESH,
        )

    def store(tile):
        lanes = pl.ds(pl.multiple_of(tile * TILE, TILE), TILE)
        return pltpu.make_async_copy(conv.at[:, :, lanes], out_ref.at[:, :, lanes], store_sem.at[tile])

    def advance(tile):
        lanes = pl.ds(pl.multiple_of(tile * TILE, TILE), TILE)
        for band in range(bands):
            index = tile * bands + band
            band_rows = slice(band * EIGHT, (band + 1) * EIGHT)

            @pl.when(takes)
            def _(index=index):
                state(index).wait_recv()

            now = [arrived[index, entry] for entry in range(4)]
            past = [arrived[index, 4 + entry] for entry in range(4)]
            for k in range(planes):
                retained = 1.0 - near_ref[slot_ref[k]]
                xx = coef[k, 0, band_rows, lanes]
                yy = coef[k, 1, band_rows, lanes]
                xy = coef[k, 2, band_rows, lanes]
                ahead = [
                    xx * now[0] + xy * now[2] + retained * past[0],
                    xx * now[1] + xy * now[3] + retained * past[1],
                    xy * now[0] + yy * now[2] + retained * past[2],
                    xy * now[1] + yy * now[3] + retained * past[3],
                ]
                now, past = ahead, now
                conv[k, band_rows, lanes] = 1.0 - 0.5 * (ahead[0] + ahead[3])
            for entry in range(4):
                leaving[index, entry] = now[entry]
                leaving[index, 4 + entry] = past[entry]

            @pl.when(gives)
            def _(index=index):
                state(index).start()

        store(tile).start()

    await_halo(0)

    def step(tile, carry):
        await_halo(2 * tile + 1)

        @pl.when(tile < tiles - 1)
        def _():
            await_halo(2 * tile + 2)

        curvature(tile)
        advance(tile)
        return carry

    lax.fori_loop(0, tiles, step, 0)

    def finish_halo(piece, carry):
        for side in (0, 1):
            @pl.when(sends[side])
            def _(side=side):
                halo(side, 0, piece).wait_send()
                halo(side, 1, piece).wait_send()
        return carry

    lax.fori_loop(0, pieces, finish_halo, 0)

    @pl.when(gives)
    def _():
        def finish(index, carry):
            state(index).wait_send()
            return carry
        lax.fori_loop(0, tiles * bands, finish, 0)

    def finish_store(tile, carry):
        store(tile).wait()
        return carry

    lax.fori_loop(0, tiles, finish_store, 0)


def per_device(potential, widths, plane_slot, ratio_near, ratio_lens):
    planes, rows, cols = potential.shape
    ninth = round_up(planes, EIGHT) // EIGHT
    wide = cols + 2 * LANES
    tall = rows + 2 * WMAX + 2 * EIGHT * ninth
    states = (cols // TILE) * (rows // EIGHT)
    smem = pl.BlockSpec(memory_space=pltpu.SMEM)
    return pl.pallas_call(
        kernel,
        out_shape=jax.ShapeDtypeStruct(potential.shape, F32),
        in_specs=[smem, smem, smem, smem, pl.BlockSpec(memory_space=pl.ANY)],
        out_specs=pl.BlockSpec(memory_space=pl.ANY),
        scratch_shapes=[
            pltpu.VMEM((planes, rows, wide), F32),
            pltpu.VMEM((planes + ninth, EIGHT, wide), F32),
            pltpu.VMEM((planes + ninth, EIGHT, wide), F32),
            pltpu.VMEM((2, ninth, EIGHT, cols), F32),
            pltpu.VMEM((planes, 3 * rows, 2 * tall), BF16),
            pltpu.VMEM((planes, 3, 3 * LANES, LANES), BF16),
            pltpu.VMEM((planes, 3, rows, cols), F32),
            pltpu.VMEM((states, 8, EIGHT, TILE), F32),
            pltpu.VMEM((states, 8, EIGHT, TILE), F32),
            pltpu.VMEM((planes, rows, cols), F32),
            pltpu.SemaphoreType.DMA,
            pltpu.SemaphoreType.DMA((2, 2, cols // LANES)),
            pltpu.SemaphoreType.DMA((2, 2, cols // LANES)),
            pltpu.SemaphoreType.DMA((states,)),
            pltpu.SemaphoreType.DMA((states,)),
            pltpu.SemaphoreType.DMA((cols // TILE,)),
        ],
        compiler_params=pltpu.CompilerParams(collective_id=0, has_side_effects=True),
        name="lensing",
    )(widths, plane_slot, ratio_near, ratio_lens, potential)


def solution(mesh):
    return jax.shard_map(
        per_device,
        mesh=mesh,
        in_specs=(P("depth", "sky", None), P("depth"), P("depth"), P(), P()),
        out_specs=P("depth", "sky", None),
        check_vma=False,
    )
```

```python
import jax
import jax.numpy as jnp
from jax import lax
from jax.experimental import pallas as pl
from jax.experimental.pallas import tpu as pltpu
from jax.sharding import PartitionSpec as P

WMAX = 8
LANES = 128
EIGHT = 8
TILE = 256
UNROLL = 6
SPAN = 128
FAR = 1000
MESH = pl.DeviceIdType.MESH
F32 = jnp.float32
BF16 = jnp.bfloat16


def round_up(value, step):
    return -(-value // step) * step


def split(values):
    high = values.astype(BF16)
    return high, (values - high.astype(F32)).astype(BF16)


def inside(distance, half_width):
    return jnp.where(jnp.abs(distance) <= half_width, 1.0, 0.0)


def kernel(
    width_ref, slot_ref, near_ref, lens_ref, pot_ref, out_ref,
    own, top, bot, pack, nears, strengths, rowm, colm, along, coef, arrived, leaving,
    load_sem, halo_send, halo_recv, state_send, state_recv,
):
    depth, sky = lax.axis_index("depth"), lax.axis_index("sky")
    has_before, has_after = sky > 0, sky < lax.axis_size("sky") - 1
    takes, gives = depth > 0, depth < lax.axis_size("depth") - 1
    planes, rows, cols = pot_ref.shape
    ninth = pack.shape[1]
    pieces, tiles, parts = cols // LANES, cols // TILE, TILE // SPAN
    units = parts * (rows // EIGHT)
    middle = pl.ds(LANES, cols)

    load = pltpu.make_async_copy(pot_ref, own.at[:, :, middle], load_sem)
    load.start()
    barrier = pltpu.get_barrier_semaphore()
    partners = (
        (has_before, {"sky": sky - 1}), (has_after, {"sky": sky + 1}),
        (takes, {"depth": depth - 1}), (gives, {"depth": depth + 1}),
    )
    for there, partner in partners:
        @pl.when(there)
        def _(partner=partner):
            pl.semaphore_signal(barrier, inc=1, device_id=partner, device_id_type=MESH)

    for buffer in (own, top, bot):
        for edge in (pl.ds(0, LANES), pl.ds(LANES + cols, LANES)):
            buffer[:, :, edge] = jnp.zeros((buffer.shape[0], buffer.shape[1], LANES), F32)
    for there, buffer in ((has_before, top), (has_after, bot)):
        @pl.when(jnp.logical_not(there))
        def _(buffer=buffer):
            buffer[...] = jnp.zeros_like(buffer)
    pack[...] = jnp.zeros_like(pack)
    load.wait()
    for side, row in ((0, rows - WMAX - 1), (1, WMAX)):
        for k in range(planes):
            pack[side, k // EIGHT, pl.ds(k % EIGHT, 1), :] = own[k, pl.ds(row, 1), middle]

    pl.semaphore_wait(barrier, sum(there.astype(jnp.int32) for there, _ in partners))

    def halo(side, part, piece):
        col = pl.multiple_of(piece * LANES, LANES)
        landing = (top, bot)[side]
        lanes_there = pl.ds(pl.multiple_of(col + LANES, LANES), LANES)
        if part == 0:
            source = pot_ref.at[:, pl.ds((rows - WMAX, 0)[side], WMAX), pl.ds(col, LANES)]
            target = landing.at[pl.ds(0, planes), :, lanes_there]
        else:
            source = pack.at[side, :, :, pl.ds(col, LANES)]
            target = landing.at[pl.ds(planes, ninth), :, lanes_there]
        return pltpu.make_async_remote_copy(
            src_ref=source, dst_ref=target,
            send_sem=halo_send.at[side, part, piece], recv_sem=halo_recv.at[side, part, piece],
            device_id={"sky": sky + (1, -1)[side]}, device_id_type=MESH,
        )

    sends, lands = (has_after, has_before), (has_before, has_after)

    def send_halo(piece, carry):
        for side in (0, 1):
            @pl.when(sends[side])
            def _(side=side):
                halo(side, 0, piece).start()
                halo(side, 1, piece).start()
        return carry

    lax.fori_loop(0, pieces, send_halo, 0)

    def await_halo(piece):
        for side in (0, 1):
            @pl.when(lands[side])
            def _(side=side):
                halo(side, 0, piece).wait_recv()
                halo(side, 1, piece).wait_recv()

    @pl.when(jnp.logical_not(takes))
    def _():
        def start(tile, carry):
            for entry in range(8):
                arrived[tile, entry] = jnp.full((EIGHT, SPAN), (1.0, 0.0, 0.0, 1.0)[entry % 4], F32)
            return carry
        lax.fori_loop(0, tiles * units, start, 0)

    own_rows = rows + 2 * WMAX
    tall = own_rows + 2 * EIGHT * ninth

    def build(k, carry):
        half_width = width_ref[k]
        share = jnp.float32(1.0 / (2 * WMAX + 1) ** 2)
        for width in range(1, WMAX):
            share = jnp.where(half_width == width, jnp.float32(1.0 / (2 * width + 1) ** 2), share)
        nears[k] = near_ref[slot_ref[k]]
        strengths[k] = lens_ref[slot_ref[k]] * share
        place = lax.broadcasted_iota(jnp.int32, (rows, 2 * tall), 1)
        place = jnp.where(place >= tall, place - tall, place)
        far_up = jnp.where(place - own_rows == k, -WMAX - 1, FAR)
        far_down = jnp.where(place - own_rows - EIGHT * ninth == k, rows + WMAX, FAR)
        row = jnp.where(place < rows, place, jnp.where(
            place < rows + WMAX, place - rows - WMAX, jnp.where(
                place < own_rows, place - WMAX, jnp.where(
                    place < own_rows + EIGHT * ninth, far_up, far_down))))
        distance = row - lax.broadcasted_iota(jnp.int32, (rows, 2 * tall), 0)
        after, here, before = (inside(distance + shift, half_width) for shift in (-1, 0, 1))
        rowm[k, 0:rows, :] = here.astype(BF16)
        rowm[k, rows:2 * rows, :] = (after - before).astype(BF16)
        rowm[k, 2 * rows:3 * rows, :] = (after - 2.0 * here + before).astype(BF16)
        shape = (2 * LANES, LANES)
        gap = lax.broadcasted_iota(jnp.int32, shape, 0) - lax.broadcasted_iota(jnp.int32, shape, 1)
        colm[k] = inside(gap - LANES // 2, half_width).astype(BF16)
        return carry

    lax.fori_loop(0, planes, build, 0)

    def along_rows(chunk):
        window = pl.ds(pl.multiple_of(chunk * TILE, TILE), TILE)

        def plane(k, carry):
            values = [own[k, :, window], top[k, :, window], bot[k, :, window]]
            values += [buffer[planes + i, :, window] for buffer in (top, bot) for i in range(ninth)]
            terms = jnp.concatenate(split(jnp.concatenate(values, axis=0)), axis=0)
            along[k, :, window] = jnp.dot(rowm[k], terms, preferred_element_type=F32)
            return carry

        lax.fori_loop(0, planes, plane, 0, unroll=UNROLL)

    def along_columns(tile):
        col = pl.multiple_of(tile * TILE, TILE)
        lane = lax.broadcasted_iota(jnp.int32, (rows, LANES), 1)

        def plane(k, carry):
            half_width, near, strength = width_ref[k], nears[k], strengths[k]

            def blocks(kind):
                return [along[k, kind * rows:(kind + 1) * rows, pl.ds(pl.multiple_of(col + i * LANES, LANES), LANES)]
                        for i in range(4)]

            def spread(values):
                turned = [pltpu.roll(value, LANES - half_width, 1) for value in values[1:]]
                ahead = [jnp.where(lane < LANES - half_width, turned[i], turned[i + 1]) for i in range(2)]
                turned = [pltpu.roll(value, half_width + 1, 1) for value in values[:-1]]
                behind = [jnp.where(lane > half_width, turned[i + 1], turned[i]) for i in range(2)]
                return jnp.concatenate([ahead[i] - behind[i] for i in range(2)], axis=1)

            def neighbours(values):
                turned = [pltpu.roll(value, LANES - 1, 1) for value in values]
                return [jnp.where(lane < LANES - 1, turned[i], turned[i + 1]) for i in range(3)] + turned[3:]

            boxed = blocks(0)
            xx = spread([after - here for after, here in zip(neighbours(boxed), boxed)])
            coef[k, 0, :, pl.ds(col, TILE)] = near - strength * xx
            slopes = blocks(1)
            xy = spread([after + here for after, here in zip(neighbours(slopes), slopes)])
            coef[k, 2, :, pl.ds(col, TILE)] = (-0.25 * strength) * xy
            turned = [pltpu.roll(value, LANES // 2, 1) for value in blocks(2)]
            halves = [jnp.where(lane < LANES // 2, turned[i], turned[i + 1]) for i in range(3)]
            terms = [split(half) for half in halves]
            stacked = jnp.concatenate([
                jnp.concatenate([terms[i][term], terms[i + 1][term]], axis=1)
                for i in range(2) for term in range(2)], axis=0)
            both = jnp.dot(stacked, colm[k], preferred_element_type=F32)
            yy = jnp.concatenate([
                both[2 * i * rows:(2 * i + 1) * rows] + both[(2 * i + 1) * rows:(2 * i + 2) * rows]
                for i in range(2)], axis=1)
            coef[k, 1, :, pl.ds(col, TILE)] = near - strength * yy
            return carry

        lax.fori_loop(0, planes, plane, 0, unroll=UNROLL)

    def state(index):
        return pltpu.make_async_remote_copy(
            src_ref=leaving.at[index], dst_ref=arrived.at[index],
            send_sem=state_send.at[index], recv_sem=state_recv.at[index],
            device_id={"depth": depth + 1}, device_id_type=MESH,
        )

    def advance(tile):
        for unit in range(units):
            index = tile * units + unit
            band, part = unit // parts, unit % parts
            band_rows = slice(band * EIGHT, (band + 1) * EIGHT)
            lanes = pl.ds(pl.multiple_of(tile * TILE + part * SPAN, SPAN), SPAN)

            @pl.when(takes)
            def _(index=index):
                state(index).wait_recv()

            now = [arrived[index, entry] for entry in range(4)]
            past = [arrived[index, 4 + entry] for entry in range(4)]
            for k in range(planes):
                retained = 1.0 - nears[k]
                xx = coef[k, 0, band_rows, lanes]
                yy = coef[k, 1, band_rows, lanes]
                xy = coef[k, 2, band_rows, lanes]
                ahead = [
                    xx * now[0] + xy * now[2] + retained * past[0],
                    xx * now[1] + xy * now[3] + retained * past[1],
                    xy * now[0] + yy * now[2] + retained * past[2],
                    xy * now[1] + yy * now[3] + retained * past[3],
                ]
                now, past = ahead, now
                out_ref[k, band_rows, lanes] = 1.0 - 0.5 * (ahead[0] + ahead[3])
            for entry in range(4):
                leaving[index, entry] = now[entry]
                leaving[index, 4 + entry] = past[entry]

            @pl.when(gives)
            def _(index=index):
                state(index).start()

    await_halo(0)
    along_rows(0)
    lead = jnp.minimum(2 * depth, tiles)

    def step(turn, carry):
        @pl.when(turn < tiles)
        def _():
            await_halo(2 * turn + 1)

            @pl.when(turn < tiles - 1)
            def _():
                await_halo(2 * turn + 2)

            along_rows(turn + 1)
            along_columns(turn)

        @pl.when((turn >= lead) & (turn - lead < tiles))
        def _():
            advance(turn - lead)

        return carry

    lax.fori_loop(0, tiles + lead, step, 0)

    def finish_halo(piece, carry):
        for side in (0, 1):
            @pl.when(sends[side])
            def _(side=side):
                halo(side, 0, piece).wait_send()
                halo(side, 1, piece).wait_send()
        return carry

    lax.fori_loop(0, pieces, finish_halo, 0)

    @pl.when(gives)
    def _():
        def finish(index, carry):
            state(index).wait_send()
            return carry
        lax.fori_loop(0, tiles * units, finish, 0)


def per_device(potential, widths, plane_slot, ratio_near, ratio_lens):
    planes, rows, cols = potential.shape
    ninth = round_up(planes, EIGHT) // EIGHT
    wide = cols + 2 * LANES
    tall = rows + 2 * WMAX + 2 * EIGHT * ninth
    states = (cols // SPAN) * (rows // EIGHT)
    smem = pl.BlockSpec(memory_space=pltpu.SMEM)
    return pl.pallas_call(
        kernel,
        out_shape=pltpu.VMEM(potential.shape, F32),
        in_specs=[smem, smem, smem, smem, pl.BlockSpec(memory_space=pl.ANY)],
        out_specs=pl.BlockSpec(memory_space=pltpu.VMEM),
        scratch_shapes=[
            pltpu.VMEM((planes, rows, wide), F32),
            pltpu.VMEM((planes + ninth, EIGHT, wide), F32),
            pltpu.VMEM((planes + ninth, EIGHT, wide), F32),
            pltpu.VMEM((2, ninth, EIGHT, cols), F32),
            pltpu.SMEM((planes,), F32),
            pltpu.SMEM((planes,), F32),
            pltpu.VMEM((planes, 3 * rows, 2 * tall), BF16),
            pltpu.VMEM((planes, 2 * LANES, LANES), BF16),
            pltpu.VMEM((planes, 3 * rows, wide), F32),
            pltpu.VMEM((planes, 3, rows, cols), F32),
            pltpu.VMEM((states, 8, EIGHT, SPAN), F32),
            pltpu.VMEM((states, 8, EIGHT, SPAN), F32),
            pltpu.SemaphoreType.DMA,
            pltpu.SemaphoreType.DMA((2, 2, cols // LANES)),
            pltpu.SemaphoreType.DMA((2, 2, cols // LANES)),
            pltpu.SemaphoreType.DMA((states,)),
            pltpu.SemaphoreType.DMA((states,)),
        ],
        compiler_params=pltpu.CompilerParams(
            collective_id=0, has_side_effects=True, vmem_limit_bytes=48 * 2**20),
        name="lensing",
    )(*(pltpu.with_memory_space_constraint(table, pltpu.HBM) for table in (widths, plane_slot, ratio_near, ratio_lens)), potential)


def solution(mesh):
    return jax.shard_map(
        per_device,
        mesh=mesh,
        in_specs=(P("depth", "sky", None), P("depth"), P("depth"), P(), P()),
        out_specs=P("depth", "sky", None),
        check_vma=False,
    )
```

```python
import jax
import jax.numpy as jnp
from jax import lax
from jax.experimental import pallas as pl
from jax.experimental.pallas import tpu as pltpu
from jax.sharding import PartitionSpec as P

WMAX = 8
LANES = 128
EIGHT = 8
TILE = 256
SPAN = 128
FAR = 1000
PAIR = 2
DETOUR = (2, 4)
MESH = pl.DeviceIdType.MESH
F32 = jnp.float32
BF16 = jnp.bfloat16


def round_up(value, step):
    return -(-value // step) * step


def split(values):
    high = values.astype(BF16)
    return high, (values - high.astype(F32)).astype(BF16)


def inside(distance, half_width):
    return jnp.where(jnp.abs(distance) <= half_width, 1.0, 0.0)


def kernel(
    width_ref, slot_ref, near_ref, lens_ref, pot_ref, out_ref,
    own, top, bot, pack, relay, nears, strengths, rowm, colm, along, coef, arrived, leaving,
    load_sem, halo_send, halo_recv, relay_send, relay_recv, forward_send, state_send, state_recv,
):
    depth, sky = lax.axis_index("depth"), lax.axis_index("sky")
    has_before, has_after = sky > 0, sky < lax.axis_size("sky") - 1
    takes, gives = depth > 0, depth < lax.axis_size("depth") - 1
    planes, rows, cols = pot_ref.shape
    ninth = pack.shape[1]
    pieces, tiles, parts = cols // LANES, cols // TILE, TILE // SPAN
    bands = rows // EIGHT
    units = parts * bands
    middle = pl.ds(LANES, cols)

    load = pltpu.make_async_copy(pot_ref, own.at[:, :, middle], load_sem)
    load.start()
    x, x_size = depth // PAIR, lax.axis_size("depth") // PAIR
    mirror = depth + PAIR * (x_size - 1 - 2 * x)
    detours, relays = x < x_size // 2, x >= x_size - x_size // 2
    at_end = (x == 0) | (x == x_size - 1)
    detoured = jnp.where(at_end, pieces // DETOUR[0], pieces // DETOUR[1])
    first = pieces - detoured
    odd = sky % 2 == 1
    leaves = (odd & has_after, jnp.logical_not(odd) & has_before)
    enters = (jnp.logical_not(odd) & has_before, odd & has_after)
    outside = leaves[0] | leaves[1]

    barrier = pltpu.get_barrier_semaphore()
    partners = (
        ((detours | relays) & outside, {"depth": mirror}),
        ((detours | relays) & leaves[0], {"depth": mirror, "sky": sky + 1}),
        ((detours | relays) & leaves[1], {"depth": mirror, "sky": sky - 1}),
        (has_before, {"sky": sky - 1}), (has_after, {"sky": sky + 1}),
        (takes, {"depth": depth - 1}), (gives, {"depth": depth + 1}),
    )
    for there, partner in partners:
        @pl.when(there)
        def _(partner=partner):
            pl.semaphore_signal(barrier, inc=1, device_id=partner, device_id_type=MESH)

    for buffer in (own, top, bot):
        for edge in (pl.ds(0, LANES), pl.ds(LANES + cols, LANES)):
            buffer[:, :, edge] = jnp.zeros((buffer.shape[0], buffer.shape[1], LANES), F32)
    for there, buffer in ((has_before, top), (has_after, bot)):
        @pl.when(jnp.logical_not(there))
        def _(buffer=buffer):
            buffer[...] = jnp.zeros_like(buffer)
    pack[...] = jnp.zeros_like(pack)
    load.wait()
    for side, row in ((0, rows - WMAX - 1), (1, WMAX)):
        for k in range(planes):
            pack[side, k // EIGHT, pl.ds(k % EIGHT, 1), :] = own[k, pl.ds(row, 1), middle]

    pl.semaphore_wait(barrier, sum(there.astype(jnp.int32) for there, _ in partners))

    def halo(side, part, piece):
        col = pl.multiple_of(piece * LANES, LANES)
        landing = (top, bot)[side]
        lanes_there = pl.ds(pl.multiple_of(col + LANES, LANES), LANES)
        if part == 0:
            source = pot_ref.at[:, pl.ds((rows - WMAX, 0)[side], WMAX), pl.ds(col, LANES)]
            target = landing.at[pl.ds(0, planes), :, lanes_there]
        else:
            source = pack.at[side, :, :, pl.ds(col, LANES)]
            target = landing.at[pl.ds(planes, ninth), :, lanes_there]
        return pltpu.make_async_remote_copy(
            src_ref=source, dst_ref=target,
            send_sem=halo_send.at[side, part, piece], recv_sem=halo_recv.at[side, part, piece],
            device_id={"sky": sky + (1, -1)[side]}, device_id_type=MESH,
        )

    sends, lands = (has_after, has_before), (has_before, has_after)

    def by_mirror(side, part, index):
        col = pl.multiple_of((first + index) * LANES, LANES)
        if part == 0:
            source = pot_ref.at[:, pl.ds((rows - WMAX, 0)[side], WMAX), pl.ds(col, LANES)]
            target = relay.at[index, pl.ds(0, planes)]
        else:
            source = pack.at[side, :, :, pl.ds(col, LANES)]
            target = relay.at[index, pl.ds(planes, ninth)]
        return pltpu.make_async_remote_copy(
            src_ref=source, dst_ref=target,
            send_sem=relay_send.at[part, index], recv_sem=relay_recv.at[part, index],
            device_id={"depth": mirror}, device_id_type=MESH,
        )

    def forward(side, index):
        piece = first + index
        lanes_there = pl.ds(pl.multiple_of(piece * LANES + LANES, LANES), LANES)
        return pltpu.make_async_remote_copy(
            src_ref=relay.at[index], dst_ref=(top, bot)[side].at[:, :, lanes_there],
            send_sem=forward_send.at[index], recv_sem=halo_recv.at[side, 0, piece],
            device_id={"depth": mirror, "sky": sky + (1, -1)[side]}, device_id_type=MESH,
        )

    def each_detoured(act):
        for side in (0, 1):
            @pl.when(detours & leaves[side])
            def _(side=side):
                def one(index, carry):
                    act(by_mirror(side, 0, index))
                    act(by_mirror(side, 1, index))
                    return carry
                lax.fori_loop(0, detoured, one, 0)

    def each_direct(act):
        def one(piece, carry):
            for side in (0, 1):
                @pl.when(sends[side] & jnp.logical_not(detours & leaves[side] & (piece >= first)))
                def _(side=side):
                    act(halo(side, 0, piece))
                    act(halo(side, 1, piece))
            return carry
        lax.fori_loop(0, pieces, one, 0)

    each_detoured(lambda copy: copy.start())
    each_direct(lambda copy: copy.start())

    def pass_on(index):
        for side in (0, 1):
            @pl.when(relays & leaves[side] & (index < detoured))
            def _(side=side):
                by_mirror(side, 0, index).wait_recv()
                by_mirror(side, 1, index).wait_recv()
                forward(side, index).start()

    def await_halo(piece):
        for side in (0, 1):
            turned = detours & enters[side] & (piece >= first)

            @pl.when(lands[side] & turned)
            def _(side=side):
                forward(side, piece - first).wait_recv()

            @pl.when(lands[side] & jnp.logical_not(turned))
            def _(side=side):
                halo(side, 0, piece).wait_recv()
                halo(side, 1, piece).wait_recv()

    @pl.when(jnp.logical_not(takes))
    def _():
        def start(tile, carry):
            for entry in range(8):
                arrived[tile, entry] = jnp.full((EIGHT, SPAN), (1.0, 0.0, 0.0, 1.0)[entry % 4], F32)
            return carry
        lax.fori_loop(0, tiles * units, start, 0)

    own_rows = rows + 2 * WMAX
    tall = own_rows + 2 * EIGHT * ninth

    def build(k, carry):
        half_width = width_ref[k]
        share = jnp.float32(1.0 / (2 * WMAX + 1) ** 2)
        for width in range(1, WMAX):
            share = jnp.where(half_width == width, jnp.float32(1.0 / (2 * width + 1) ** 2), share)
        nears[k] = near_ref[slot_ref[k]]
        strengths[k] = lens_ref[slot_ref[k]] * share
        place = lax.broadcasted_iota(jnp.int32, (rows, 2 * tall), 1)
        place = jnp.where(place >= tall, place - tall, place)
        far_up = jnp.where(place - own_rows == k, -WMAX - 1, FAR)
        far_down = jnp.where(place - own_rows - EIGHT * ninth == k, rows + WMAX, FAR)
        row = jnp.where(place < rows, place, jnp.where(
            place < rows + WMAX, place - rows - WMAX, jnp.where(
                place < own_rows, place - WMAX, jnp.where(
                    place < own_rows + EIGHT * ninth, far_up, far_down))))
        distance = row - lax.broadcasted_iota(jnp.int32, (rows, 2 * tall), 0)
        after, here, before = (inside(distance + shift, half_width) for shift in (-1, 0, 1))
        rowm[k, 0:rows, :] = here.astype(BF16)
        rowm[k, rows:2 * rows, :] = (after - before).astype(BF16)
        rowm[k, 2 * rows:3 * rows, :] = (after - 2.0 * here + before).astype(BF16)
        shape = (2 * LANES, LANES)
        gap = lax.broadcasted_iota(jnp.int32, shape, 0) - lax.broadcasted_iota(jnp.int32, shape, 1)
        colm[k] = inside(gap - LANES // 2, half_width).astype(BF16)
        return carry

    lax.fori_loop(0, planes, build, 0)

    def along_rows(chunk, k):
        window = pl.ds(pl.multiple_of(chunk * TILE, TILE), TILE)
        values = [own[k, :, window], top[k, :, window], bot[k, :, window]]
        values += [buffer[planes + i, :, window] for buffer in (top, bot) for i in range(ninth)]
        terms = jnp.concatenate(split(jnp.concatenate(values, axis=0)), axis=0)
        along[k, :, window] = jnp.dot(rowm[k], terms, preferred_element_type=F32)

    def along_columns(tile, k):
        col = pl.multiple_of(tile * TILE, TILE)
        lane = lax.broadcasted_iota(jnp.int32, (rows, LANES), 1)

        half_width, near, strength = width_ref[k], nears[k], strengths[k]

        def blocks(kind):
            return [along[k, kind * rows:(kind + 1) * rows, pl.ds(pl.multiple_of(col + i * LANES, LANES), LANES)]
                    for i in range(4)]

        def spread(values):
            turned = [pltpu.roll(value, LANES - half_width, 1) for value in values[1:]]
            ahead = [jnp.where(lane < LANES - half_width, turned[i], turned[i + 1]) for i in range(2)]
            turned = [pltpu.roll(value, half_width + 1, 1) for value in values[:-1]]
            behind = [jnp.where(lane > half_width, turned[i + 1], turned[i]) for i in range(2)]
            return jnp.concatenate([ahead[i] - behind[i] for i in range(2)], axis=1)

        def neighbours(values):
            turned = [pltpu.roll(value, LANES - 1, 1) for value in values]
            return [jnp.where(lane < LANES - 1, turned[i], turned[i + 1]) for i in range(3)] + turned[3:]

        boxed = blocks(0)
        xx = spread([after - here for after, here in zip(neighbours(boxed), boxed)])
        coef[k, 0, :, pl.ds(col, TILE)] = near - strength * xx
        slopes = blocks(1)
        xy = spread([after + here for after, here in zip(neighbours(slopes), slopes)])
        coef[k, 2, :, pl.ds(col, TILE)] = (-0.25 * strength) * xy
        turned = [pltpu.roll(value, LANES // 2, 1) for value in blocks(2)]
        halves = [jnp.where(lane < LANES // 2, turned[i], turned[i + 1]) for i in range(3)]
        terms = [split(half) for half in halves]
        stacked = jnp.concatenate([
            jnp.concatenate([terms[i][term], terms[i + 1][term]], axis=1)
            for i in range(2) for term in range(2)], axis=0)
        both = jnp.dot(stacked, colm[k], preferred_element_type=F32)
        yy = jnp.concatenate([
            both[2 * i * rows:(2 * i + 1) * rows] + both[(2 * i + 1) * rows:(2 * i + 2) * rows]
            for i in range(2)], axis=1)
        coef[k, 1, :, pl.ds(col, TILE)] = near - strength * yy

    def state(index):
        return pltpu.make_async_remote_copy(
            src_ref=leaving.at[index], dst_ref=arrived.at[index],
            send_sem=state_send.at[index], recv_sem=state_recv.at[index],
            device_id={"depth": depth + 1}, device_id_type=MESH,
        )

    def advance(tile, band):
        for part in range(parts):
            index = tile * units + band * parts + part
            band_rows = pl.ds(pl.multiple_of(band * EIGHT, EIGHT), EIGHT)
            lanes = pl.ds(pl.multiple_of(tile * TILE + part * SPAN, SPAN), SPAN)

            @pl.when(takes)
            def _(index=index):
                state(index).wait_recv()

            now = [arrived[index, entry] for entry in range(4)]
            past = [arrived[index, 4 + entry] for entry in range(4)]
            for k in range(planes):
                retained = 1.0 - nears[k]
                xx = coef[k, 0, band_rows, lanes]
                yy = coef[k, 1, band_rows, lanes]
                xy = coef[k, 2, band_rows, lanes]
                ahead = [
                    xx * now[0] + xy * now[2] + retained * past[0],
                    xx * now[1] + xy * now[3] + retained * past[1],
                    xy * now[0] + yy * now[2] + retained * past[2],
                    xy * now[1] + yy * now[3] + retained * past[3],
                ]
                now, past = ahead, now
                out_ref[k, band_rows, lanes] = 1.0 - 0.5 * (ahead[0] + ahead[3])
            for entry in range(4):
                leaving[index, entry] = now[entry]
                leaving[index, 4 + entry] = past[entry]

            @pl.when(gives)
            def _(index=index):
                state(index).start()

    await_halo(0)

    def rows_first(k, carry):
        along_rows(0, k)
        return carry

    lax.fori_loop(0, planes, rows_first, 0, unroll=4)
    lead = jnp.clip(depth, 1, tiles)

    def step(turn, carry):
        builds, moves = turn < tiles, turn >= lead

        @pl.when(builds)
        def _():
            await_halo(2 * turn + 1)

            @pl.when(turn < tiles - 1)
            def _():
                await_halo(2 * turn + 2)

        def share(band, carry):
            @pl.when(moves)
            def _():
                advance(turn - lead, band)

            @pl.when(builds)
            def _():
                group = range(planes // bands)
                for i in group:
                    along_rows(turn + 1, band * len(group) + i)
                for i in group:
                    along_columns(turn, band * len(group) + i)

            return carry

        lax.fori_loop(0, bands, share, 0)

        @pl.when(builds)
        def _():
            pass_on(turn)

        return carry

    lax.fori_loop(0, tiles + lead, step, 0)

    each_detoured(lambda copy: copy.wait_send())
    each_direct(lambda copy: copy.wait_send())

    @pl.when(relays & outside)
    def _():
        def finish(index, carry):
            forward(0, index).wait_send()
            return carry
        lax.fori_loop(0, detoured, finish, 0)

    @pl.when(gives)
    def _():
        def finish(index, carry):
            state(index).wait_send()
            return carry
        lax.fori_loop(0, tiles * units, finish, 0)


def per_device(potential, widths, plane_slot, ratio_near, ratio_lens):
    planes, rows, cols = potential.shape
    ninth = round_up(planes, EIGHT) // EIGHT
    wide = cols + 2 * LANES
    tall = rows + 2 * WMAX + 2 * EIGHT * ninth
    states = (cols // SPAN) * (rows // EIGHT)
    smem = pl.BlockSpec(memory_space=pltpu.SMEM)
    return pl.pallas_call(
        kernel,
        out_shape=pltpu.VMEM(potential.shape, F32),
        in_specs=[smem, smem, smem, smem, pl.BlockSpec(memory_space=pl.ANY)],
        out_specs=pl.BlockSpec(memory_space=pltpu.VMEM),
        scratch_shapes=[
            pltpu.VMEM((planes, rows, wide), F32),
            pltpu.VMEM((planes + ninth, EIGHT, wide), F32),
            pltpu.VMEM((planes + ninth, EIGHT, wide), F32),
            pltpu.VMEM((2, ninth, EIGHT, cols), F32),
            pltpu.VMEM((max(1, cols // LANES // DETOUR[0]), planes + ninth, EIGHT, LANES), F32),
            pltpu.SMEM((planes,), F32),
            pltpu.SMEM((planes,), F32),
            pltpu.VMEM((planes, 3 * rows, 2 * tall), BF16),
            pltpu.VMEM((planes, 2 * LANES, LANES), BF16),
            pltpu.VMEM((planes, 3 * rows, wide), F32),
            pltpu.VMEM((planes, 3, rows, cols), F32),
            pltpu.VMEM((states, 8, EIGHT, SPAN), F32),
            pltpu.VMEM((states, 8, EIGHT, SPAN), F32),
            pltpu.SemaphoreType.DMA,
            pltpu.SemaphoreType.DMA((2, 2, cols // LANES)),
            pltpu.SemaphoreType.DMA((2, 2, cols // LANES)),
            pltpu.SemaphoreType.DMA((2, max(1, cols // LANES // DETOUR[0]))),
            pltpu.SemaphoreType.DMA((2, max(1, cols // LANES // DETOUR[0]))),
            pltpu.SemaphoreType.DMA((max(1, cols // LANES // DETOUR[0]),)),
            pltpu.SemaphoreType.DMA((states,)),
            pltpu.SemaphoreType.DMA((states,)),
        ],
        compiler_params=pltpu.CompilerParams(
            collective_id=0, has_side_effects=True, vmem_limit_bytes=48 * 2**20),
        name="lensing",
    )(*(pltpu.with_memory_space_constraint(table, pltpu.HBM) for table in (widths, plane_slot, ratio_near, ratio_lens)), potential)


def solution(mesh):
    return jax.shard_map(
        per_device,
        mesh=mesh,
        in_specs=(P("depth", "sky", None), P("depth"), P("depth"), P(), P()),
        out_specs=P("depth", "sky", None),
        check_vma=False,
    )
```

```python
import jax
import jax.numpy as jnp
from jax import lax
from jax.experimental import pallas as pl
from jax.experimental.pallas import tpu as pltpu
from jax.sharding import PartitionSpec as P

WMAX = 8
LANES = 128
EIGHT = 8
TILE = 256
SPAN = 128
FAR = 1000
PAIR = 2
DETOUR = (6, 3)
MESH = pl.DeviceIdType.MESH
F32 = jnp.float32
BF16 = jnp.bfloat16


def round_up(value, step):
    return -(-value // step) * step


def split(values):
    high = values.astype(BF16)
    return high, (values - high.astype(F32)).astype(BF16)


def inside(distance, half_width):
    return jnp.where(jnp.abs(distance) <= half_width, 1.0, 0.0)


def kernel(
    width_hbm, slot_hbm, near_hbm, lens_hbm, pot_ref, out_ref,
    width_ref, slot_ref, near_ref, lens_ref, own, top, bot, pack, relay, nears, strengths, rowm, colm, along, coef, arrived, leaving,
    load_sem, table_sem, halo_send, halo_recv, relay_send, relay_recv, forward_send, state_send, state_recv,
):
    depth, sky = lax.axis_index("depth"), lax.axis_index("sky")
    has_before, has_after = sky > 0, sky < lax.axis_size("sky") - 1
    takes, gives = depth > 0, depth < lax.axis_size("depth") - 1
    planes, rows, cols = pot_ref.shape
    ninth = pack.shape[1]
    pieces, tiles, parts = cols // LANES, cols // TILE, TILE // SPAN
    bands = rows // EIGHT
    units = parts * bands
    middle = pl.ds(LANES, cols)

    edges = ((WMAX, rows - 2 * WMAX), (0, WMAX), (rows - WMAX, WMAX))
    loads = [
        pltpu.make_async_copy(pot_ref.at[:, pl.ds(*part), :], own.at[:, pl.ds(*part), middle], load_sem.at[i])
        for i, part in enumerate(edges)]
    tables = [
        pltpu.make_async_copy(*pair, table_sem.at[i]) for i, pair in enumerate((
            (width_hbm, width_ref), (slot_hbm, slot_ref), (near_hbm, near_ref), (lens_hbm, lens_ref)))]
    for copy in loads + tables:
        copy.start()
    x, x_size = depth // PAIR, lax.axis_size("depth") // PAIR
    mirror = depth + PAIR * (x_size - 1 - 2 * x)
    detours, relays = x < x_size // 2, x >= x_size - x_size // 2
    at_end = (x == 0) | (x == x_size - 1)
    detoured = jnp.where(at_end, pieces * DETOUR[0] // 16, pieces * DETOUR[1] // 16)
    first = pieces - detoured
    odd = sky % 2 == 1
    leaves = (odd & has_after, jnp.logical_not(odd) & has_before)
    enters = (jnp.logical_not(odd) & has_before, odd & has_after)
    outside = leaves[0] | leaves[1]

    barrier = pltpu.get_barrier_semaphore()
    partners = (
        ((detours | relays) & outside, {"depth": mirror}),
        ((detours | relays) & leaves[0], {"depth": mirror, "sky": sky + 1}),
        ((detours | relays) & leaves[1], {"depth": mirror, "sky": sky - 1}),
        (has_before, {"sky": sky - 1}), (has_after, {"sky": sky + 1}),
        (takes, {"depth": depth - 1}), (gives, {"depth": depth + 1}),
    )
    for there, partner in partners:
        @pl.when(there)
        def _(partner=partner):
            pl.semaphore_signal(barrier, inc=1, device_id=partner, device_id_type=MESH)

    for buffer in (own, top, bot):
        for edge in (pl.ds(0, LANES), pl.ds(LANES + cols, LANES)):
            buffer[:, :, edge] = jnp.zeros((buffer.shape[0], buffer.shape[1], LANES), F32)
    for there, buffer in ((has_before, top), (has_after, bot)):
        @pl.when(jnp.logical_not(there))
        def _(buffer=buffer):
            buffer[...] = jnp.zeros_like(buffer)
    pack[...] = jnp.zeros_like(pack)
    loads[0].wait()
    for side, row in ((0, rows - WMAX - 1), (1, WMAX)):
        for k in range(planes):
            pack[side, k // EIGHT, pl.ds(k % EIGHT, 1), :] = own[k, pl.ds(row, 1), middle]

    pl.semaphore_wait(barrier, sum(there.astype(jnp.int32) for there, _ in partners))

    def halo(side, part, piece):
        col = pl.multiple_of(piece * LANES, LANES)
        landing = (top, bot)[side]
        lanes_there = pl.ds(pl.multiple_of(col + LANES, LANES), LANES)
        if part == 0:
            source = pot_ref.at[:, pl.ds((rows - WMAX, 0)[side], WMAX), pl.ds(col, LANES)]
            target = landing.at[pl.ds(0, planes), :, lanes_there]
        else:
            source = pack.at[side, :, :, pl.ds(col, LANES)]
            target = landing.at[pl.ds(planes, ninth), :, lanes_there]
        return pltpu.make_async_remote_copy(
            src_ref=source, dst_ref=target,
            send_sem=halo_send.at[side, part, piece], recv_sem=halo_recv.at[side, part, piece],
            device_id={"sky": sky + (1, -1)[side]}, device_id_type=MESH,
        )

    sends, lands = (has_after, has_before), (has_before, has_after)

    def by_mirror(side, part, index):
        col = pl.multiple_of((first + index) * LANES, LANES)
        if part == 0:
            source = pot_ref.at[:, pl.ds((rows - WMAX, 0)[side], WMAX), pl.ds(col, LANES)]
            target = relay.at[index, pl.ds(0, planes)]
        else:
            source = pack.at[side, :, :, pl.ds(col, LANES)]
            target = relay.at[index, pl.ds(planes, ninth)]
        return pltpu.make_async_remote_copy(
            src_ref=source, dst_ref=target,
            send_sem=relay_send.at[part, index], recv_sem=relay_recv.at[part, index],
            device_id={"depth": mirror}, device_id_type=MESH,
        )

    def forward(side, index):
        piece = first + index
        lanes_there = pl.ds(pl.multiple_of(piece * LANES + LANES, LANES), LANES)
        return pltpu.make_async_remote_copy(
            src_ref=relay.at[index], dst_ref=(top, bot)[side].at[:, :, lanes_there],
            send_sem=forward_send.at[index], recv_sem=halo_recv.at[side, 0, piece],
            device_id={"depth": mirror, "sky": sky + (1, -1)[side]}, device_id_type=MESH,
        )

    def each_detoured(act):
        for side in (0, 1):
            @pl.when(detours & leaves[side])
            def _(side=side):
                def one(index, carry):
                    act(by_mirror(side, 0, index))
                    act(by_mirror(side, 1, index))
                    return carry
                lax.fori_loop(0, detoured, one, 0)

    def direct(piece, act):
        for side in (0, 1):
            @pl.when(sends[side] & jnp.logical_not(detours & leaves[side] & (piece >= first)))
            def _(side=side):
                act(halo(side, 0, piece))
                act(halo(side, 1, piece))

    def each_direct(act, count):
        def one(piece, carry):
            direct(piece, act)
            return carry
        lax.fori_loop(0, count, one, 0)

    each_detoured(lambda copy: copy.start())
    early = jnp.where(relays & at_end, pieces // 2, pieces)
    each_direct(lambda copy: copy.start(), early)

    def pass_on(index):
        for side in (0, 1):
            @pl.when(relays & leaves[side] & (index < detoured))
            def _(side=side):
                by_mirror(side, 0, index).wait_recv()
                by_mirror(side, 1, index).wait_recv()
                forward(side, index).start()

    def await_halo(piece):
        for side in (0, 1):
            turned = detours & enters[side] & (piece >= first)

            @pl.when(lands[side] & turned)
            def _(side=side):
                forward(side, piece - first).wait_recv()

            @pl.when(lands[side] & jnp.logical_not(turned))
            def _(side=side):
                halo(side, 0, piece).wait_recv()
                halo(side, 1, piece).wait_recv()

    @pl.when(jnp.logical_not(takes))
    def _():
        def start(tile, carry):
            for entry in range(8):
                arrived[tile, entry] = jnp.full((EIGHT, SPAN), (1.0, 0.0, 0.0, 1.0)[entry % 4], F32)
            return carry
        lax.fori_loop(0, tiles * units, start, 0)

    own_rows = rows + 2 * WMAX
    tall = own_rows + 2 * EIGHT * ninth

    def build(k, carry):
        half_width = width_ref[k]
        share = jnp.float32(1.0 / (2 * WMAX + 1) ** 2)
        for width in range(1, WMAX):
            share = jnp.where(half_width == width, jnp.float32(1.0 / (2 * width + 1) ** 2), share)
        nears[k] = near_ref[slot_ref[k]]
        strengths[k] = lens_ref[slot_ref[k]] * share
        place = lax.broadcasted_iota(jnp.int32, (rows, 2 * tall), 1)
        place = jnp.where(place >= tall, place - tall, place)
        far_up = jnp.where(place - own_rows == k, -WMAX - 1, FAR)
        far_down = jnp.where(place - own_rows - EIGHT * ninth == k, rows + WMAX, FAR)
        row = jnp.where(place < rows, place, jnp.where(
            place < rows + WMAX, place - rows - WMAX, jnp.where(
                place < own_rows, place - WMAX, jnp.where(
                    place < own_rows + EIGHT * ninth, far_up, far_down))))
        distance = row - lax.broadcasted_iota(jnp.int32, (rows, 2 * tall), 0)
        after, here, before = (inside(distance + shift, half_width) for shift in (-1, 0, 1))
        rowm[k, 0:rows, :] = here.astype(BF16)
        rowm[k, rows:2 * rows, :] = (after - before).astype(BF16)
        rowm[k, 2 * rows:3 * rows, :] = (after - 2.0 * here + before).astype(BF16)
        shape = (2 * LANES, LANES)
        gap = lax.broadcasted_iota(jnp.int32, shape, 0) - lax.broadcasted_iota(jnp.int32, shape, 1)
        colm[k] = inside(gap - LANES // 2, half_width).astype(BF16)
        return carry

    for copy in tables:
        copy.wait()
    lax.fori_loop(0, planes, build, 0)
    for copy in loads[1:]:
        copy.wait()

    def along_rows(chunk, k):
        window = pl.ds(pl.multiple_of(chunk * TILE, TILE), TILE)
        values = [own[k, :, window], top[k, :, window], bot[k, :, window]]
        values += [buffer[planes + i, :, window] for buffer in (top, bot) for i in range(ninth)]
        terms = jnp.concatenate(split(jnp.concatenate(values, axis=0)), axis=0)
        along[k, :, window] = jnp.dot(rowm[k], terms, preferred_element_type=F32)

    def along_columns(tile, k):
        col = pl.multiple_of(tile * TILE, TILE)
        lane = lax.broadcasted_iota(jnp.int32, (rows, LANES), 1)

        half_width, near, strength = width_ref[k], nears[k], strengths[k]

        def blocks(kind):
            return [along[k, kind * rows:(kind + 1) * rows, pl.ds(pl.multiple_of(col + i * LANES, LANES), LANES)]
                    for i in range(4)]

        def spread(values):
            turned = [pltpu.roll(value, LANES - half_width, 1) for value in values[1:]]
            ahead = [jnp.where(lane < LANES - half_width, turned[i], turned[i + 1]) for i in range(2)]
            turned = [pltpu.roll(value, half_width + 1, 1) for value in values[:-1]]
            behind = [jnp.where(lane > half_width, turned[i + 1], turned[i]) for i in range(2)]
            return jnp.concatenate([ahead[i] - behind[i] for i in range(2)], axis=1)

        def neighbours(values):
            turned = [pltpu.roll(value, LANES - 1, 1) for value in values]
            return [jnp.where(lane < LANES - 1, turned[i], turned[i + 1]) for i in range(3)] + turned[3:]

        boxed = blocks(0)
        xx = spread([after - here for after, here in zip(neighbours(boxed), boxed)])
        coef[k, 0, :, pl.ds(col, TILE)] = near - strength * xx
        slopes = blocks(1)
        xy = spread([after + here for after, here in zip(neighbours(slopes), slopes)])
        coef[k, 2, :, pl.ds(col, TILE)] = (-0.25 * strength) * xy
        turned = [pltpu.roll(value, LANES // 2, 1) for value in blocks(2)]
        halves = [jnp.where(lane < LANES // 2, turned[i], turned[i + 1]) for i in range(3)]
        terms = [split(half) for half in halves]
        stacked = jnp.concatenate([
            jnp.concatenate([terms[i][term], terms[i + 1][term]], axis=1)
            for i in range(2) for term in range(2)], axis=0)
        both = jnp.dot(stacked, colm[k], preferred_element_type=F32)
        yy = jnp.concatenate([
            both[2 * i * rows:(2 * i + 1) * rows] + both[(2 * i + 1) * rows:(2 * i + 2) * rows]
            for i in range(2)], axis=1)
        coef[k, 1, :, pl.ds(col, TILE)] = near - strength * yy

    def state(index):
        return pltpu.make_async_remote_copy(
            src_ref=leaving.at[index], dst_ref=arrived.at[index],
            send_sem=state_send.at[index], recv_sem=state_recv.at[index],
            device_id={"depth": depth + 1}, device_id_type=MESH,
        )

    def advance(tile, band):
        for part in range(parts):
            index = tile * units + band * parts + part
            band_rows = pl.ds(pl.multiple_of(band * EIGHT, EIGHT), EIGHT)
            lanes = pl.ds(pl.multiple_of(tile * TILE + part * SPAN, SPAN), SPAN)

            @pl.when(takes)
            def _(index=index):
                state(index).wait_recv()

            now = [arrived[index, entry] for entry in range(4)]
            past = [arrived[index, 4 + entry] for entry in range(4)]
            for k in range(planes):
                retained = 1.0 - nears[k]
                xx = coef[k, 0, band_rows, lanes]
                yy = coef[k, 1, band_rows, lanes]
                xy = coef[k, 2, band_rows, lanes]
                ahead = [
                    xx * now[0] + xy * now[2] + retained * past[0],
                    xx * now[1] + xy * now[3] + retained * past[1],
                    xy * now[0] + yy * now[2] + retained * past[2],
                    xy * now[1] + yy * now[3] + retained * past[3],
                ]
                now, past = ahead, now
                out_ref[k, band_rows, lanes] = 1.0 - 0.5 * (ahead[0] + ahead[3])
            for entry in range(4):
                leaving[index, entry] = now[entry]
                leaving[index, 4 + entry] = past[entry]

            @pl.when(gives)
            def _(index=index):
                state(index).start()

    await_halo(0)

    def rows_first(k, carry):
        along_rows(0, k)
        return carry

    lax.fori_loop(0, planes, rows_first, 0, unroll=4)
    lead = jnp.clip(depth, 1, tiles)

    def step(turn, carry):
        builds, moves = turn < tiles, turn >= lead

        @pl.when(builds)
        def _():
            await_halo(2 * turn + 1)

            @pl.when(turn < tiles - 1)
            def _():
                await_halo(2 * turn + 2)

        def share(band, carry):
            @pl.when(moves)
            def _():
                advance(turn - lead, band)

            @pl.when(builds)
            def _():
                group = range(planes // bands)
                for i in group:
                    along_rows(turn + 1, band * len(group) + i)
                for i in group:
                    along_columns(turn, band * len(group) + i)

            return carry

        lax.fori_loop(0, bands, share, 0)

        @pl.when(builds)
        def _():
            pass_on(2 * turn)
            pass_on(2 * turn + 1)
            for later in (early + 2 * turn, early + 2 * turn + 1):
                @pl.when(later < pieces)
                def _(later=later):
                    direct(later, lambda copy: copy.start())

        return carry

    lax.fori_loop(0, tiles + lead, step, 0)

    each_detoured(lambda copy: copy.wait_send())
    each_direct(lambda copy: copy.wait_send(), pieces)

    @pl.when(relays & outside)
    def _():
        def finish(index, carry):
            forward(0, index).wait_send()
            return carry
        lax.fori_loop(0, detoured, finish, 0)

    @pl.when(gives)
    def _():
        def finish(index, carry):
            state(index).wait_send()
            return carry
        lax.fori_loop(0, tiles * units, finish, 0)


def per_device(potential, widths, plane_slot, ratio_near, ratio_lens):
    planes, rows, cols = potential.shape
    ninth = round_up(planes, EIGHT) // EIGHT
    wide = cols + 2 * LANES
    tall = rows + 2 * WMAX + 2 * EIGHT * ninth
    states = (cols // SPAN) * (rows // EIGHT)
    table = ratio_near.shape[0]
    return pl.pallas_call(
        kernel,
        out_shape=pltpu.VMEM(potential.shape, F32),
        in_specs=[pl.BlockSpec(memory_space=pl.ANY)] * 5,
        out_specs=pl.BlockSpec(memory_space=pltpu.VMEM),
        scratch_shapes=[
            pltpu.SMEM((planes,), jnp.int32),
            pltpu.SMEM((planes,), jnp.int32),
            pltpu.SMEM((table,), F32),
            pltpu.SMEM((table,), F32),
            pltpu.VMEM((planes, rows, wide), F32),
            pltpu.VMEM((planes + ninth, EIGHT, wide), F32),
            pltpu.VMEM((planes + ninth, EIGHT, wide), F32),
            pltpu.VMEM((2, ninth, EIGHT, cols), F32),
            pltpu.VMEM((max(1, cols // LANES * DETOUR[0] // 16), planes + ninth, EIGHT, LANES), F32),
            pltpu.SMEM((planes,), F32),
            pltpu.SMEM((planes,), F32),
            pltpu.VMEM((planes, 3 * rows, 2 * tall), BF16),
            pltpu.VMEM((planes, 2 * LANES, LANES), BF16),
            pltpu.VMEM((planes, 3 * rows, wide), F32),
            pltpu.VMEM((planes, 3, rows, cols), F32),
            pltpu.VMEM((states, 8, EIGHT, SPAN), F32),
            pltpu.VMEM((states, 8, EIGHT, SPAN), F32),
            pltpu.SemaphoreType.DMA((3,)),
            pltpu.SemaphoreType.DMA((4,)),
            pltpu.SemaphoreType.DMA((2, 2, cols // LANES)),
            pltpu.SemaphoreType.DMA((2, 2, cols // LANES)),
            pltpu.SemaphoreType.DMA((2, max(1, cols // LANES * DETOUR[0] // 16))),
            pltpu.SemaphoreType.DMA((2, max(1, cols // LANES * DETOUR[0] // 16))),
            pltpu.SemaphoreType.DMA((max(1, cols // LANES * DETOUR[0] // 16),)),
            pltpu.SemaphoreType.DMA((states,)),
            pltpu.SemaphoreType.DMA((states,)),
        ],
        compiler_params=pltpu.CompilerParams(
            collective_id=0, has_side_effects=True, vmem_limit_bytes=48 * 2**20),
        name="lensing",
    )(*(pltpu.with_memory_space_constraint(table, pltpu.HBM) for table in (widths, plane_slot, ratio_near, ratio_lens)), potential)


def solution(mesh):
    return jax.shard_map(
        per_device,
        mesh=mesh,
        in_specs=(P("depth", "sky", None), P("depth"), P("depth"), P(), P()),
        out_specs=P("depth", "sky", None),
        check_vma=False,
    )
```

```python
import jax
import jax.numpy as jnp
from jax import lax
from jax.experimental import pallas as pl
from jax.experimental.pallas import tpu as pltpu
from jax.sharding import PartitionSpec as P

WMAX = 8
LANES = 128
EIGHT = 8
TILE = 256
SPAN = 128
FAR = 1000
PAIR = 2
DETOUR = (6, 3)
MESH = pl.DeviceIdType.MESH
F32 = jnp.float32
BF16 = jnp.bfloat16


def round_up(value, step):
    return -(-value // step) * step


def split(values):
    high = values.astype(BF16)
    return high, (values - high.astype(F32)).astype(BF16)


def inside(distance, half_width):
    return jnp.where(jnp.abs(distance) <= half_width, 1.0, 0.0)


def kernel(
    width_hbm, slot_hbm, near_hbm, lens_hbm, pot_ref, out_ref,
    width_ref, slot_ref, near_ref, lens_ref, own, top, bot, pack, relay, nears, strengths, rowm, colm, along, coef, arrived, leaving,
    load_sem, table_sem, halo_send, halo_recv, relay_send, relay_recv, forward_send, state_send, state_recv,
):
    depth, sky = lax.axis_index("depth"), lax.axis_index("sky")
    has_before, has_after = sky > 0, sky < lax.axis_size("sky") - 1
    takes, gives = depth > 0, depth < lax.axis_size("depth") - 1
    planes, rows, cols = pot_ref.shape
    ninth = pack.shape[1]
    pieces, tiles, parts = cols // LANES, cols // TILE, TILE // SPAN
    bands = rows // EIGHT
    units = parts * bands
    middle = pl.ds(LANES, cols)

    edges = ((WMAX, rows - 2 * WMAX), (0, WMAX), (rows - WMAX, WMAX))
    loads = [
        pltpu.make_async_copy(pot_ref.at[:, pl.ds(*part), :], own.at[:, pl.ds(*part), middle], load_sem.at[i])
        for i, part in enumerate(edges)]
    tables = [
        pltpu.make_async_copy(*pair, table_sem.at[i]) for i, pair in enumerate((
            (width_hbm, width_ref), (slot_hbm, slot_ref), (near_hbm, near_ref), (lens_hbm, lens_ref)))]
    for copy in loads + tables:
        copy.start()
    x, x_size = depth // PAIR, lax.axis_size("depth") // PAIR
    mirror = depth + PAIR * (x_size - 1 - 2 * x)
    detours, relays = x < x_size // 2, x >= x_size - x_size // 2
    at_end = (x == 0) | (x == x_size - 1)
    detoured = jnp.where(at_end, pieces * DETOUR[0] // 16, pieces * DETOUR[1] // 16)
    first = pieces - detoured
    odd = sky % 2 == 1
    leaves = (odd & has_after, jnp.logical_not(odd) & has_before)
    enters = (jnp.logical_not(odd) & has_before, odd & has_after)
    outside = leaves[0] | leaves[1]

    barrier = pltpu.get_barrier_semaphore()
    partners = (
        ((detours | relays) & outside, {"depth": mirror}),
        ((detours | relays) & leaves[0], {"depth": mirror, "sky": sky + 1}),
        ((detours | relays) & leaves[1], {"depth": mirror, "sky": sky - 1}),
        (has_before, {"sky": sky - 1}), (has_after, {"sky": sky + 1}),
        (takes, {"depth": depth - 1}), (gives, {"depth": depth + 1}),
    )
    for there, partner in partners:
        @pl.when(there)
        def _(partner=partner):
            pl.semaphore_signal(barrier, inc=1, device_id=partner, device_id_type=MESH)

    for buffer in (own, top, bot):
        for edge in (pl.ds(0, LANES), pl.ds(LANES + cols, LANES)):
            buffer[:, :, edge] = jnp.zeros((buffer.shape[0], buffer.shape[1], LANES), F32)
    for there, buffer in ((has_before, top), (has_after, bot)):
        @pl.when(jnp.logical_not(there))
        def _(buffer=buffer):
            buffer[...] = jnp.zeros_like(buffer)
    pack[...] = jnp.zeros_like(pack)
    loads[0].wait()
    for side, row in ((0, rows - WMAX - 1), (1, WMAX)):
        for k in range(planes):
            pack[side, k // EIGHT, pl.ds(k % EIGHT, 1), :] = own[k, pl.ds(row, 1), middle]

    pl.semaphore_wait(barrier, sum(there.astype(jnp.int32) for there, _ in partners))

    def halo(side, part, piece):
        col = pl.multiple_of(piece * LANES, LANES)
        landing = (top, bot)[side]
        lanes_there = pl.ds(pl.multiple_of(col + LANES, LANES), LANES)
        if part == 0:
            source = pot_ref.at[:, pl.ds((rows - WMAX, 0)[side], WMAX), pl.ds(col, LANES)]
            target = landing.at[pl.ds(0, planes), :, lanes_there]
        else:
            source = pack.at[side, :, :, pl.ds(col, LANES)]
            target = landing.at[pl.ds(planes, ninth), :, lanes_there]
        return pltpu.make_async_remote_copy(
            src_ref=source, dst_ref=target,
            send_sem=halo_send.at[side, part, piece], recv_sem=halo_recv.at[side, part, piece],
            device_id={"sky": sky + (1, -1)[side]}, device_id_type=MESH,
        )

    sends, lands = (has_after, has_before), (has_before, has_after)

    def by_mirror(side, part, index):
        col = pl.multiple_of((first + index) * LANES, LANES)
        if part == 0:
            source = pot_ref.at[:, pl.ds((rows - WMAX, 0)[side], WMAX), pl.ds(col, LANES)]
            target = relay.at[index, pl.ds(0, planes)]
        else:
            source = pack.at[side, :, :, pl.ds(col, LANES)]
            target = relay.at[index, pl.ds(planes, ninth)]
        return pltpu.make_async_remote_copy(
            src_ref=source, dst_ref=target,
            send_sem=relay_send.at[part, index], recv_sem=relay_recv.at[part, index],
            device_id={"depth": mirror}, device_id_type=MESH,
        )

    def forward(side, index):
        piece = first + index
        lanes_there = pl.ds(pl.multiple_of(piece * LANES + LANES, LANES), LANES)
        return pltpu.make_async_remote_copy(
            src_ref=relay.at[index], dst_ref=(top, bot)[side].at[:, :, lanes_there],
            send_sem=forward_send.at[index], recv_sem=halo_recv.at[side, 0, piece],
            device_id={"depth": mirror, "sky": sky + (1, -1)[side]}, device_id_type=MESH,
        )

    def each_detoured(act):
        for side in (0, 1):
            @pl.when(detours & leaves[side])
            def _(side=side):
                def one(index, carry):
                    act(by_mirror(side, 0, index))
                    act(by_mirror(side, 1, index))
                    return carry
                lax.fori_loop(0, detoured, one, 0)

    def direct(piece, act):
        for side in (0, 1):
            @pl.when(sends[side] & jnp.logical_not(detours & leaves[side] & (piece >= first)))
            def _(side=side):
                act(halo(side, 0, piece))
                act(halo(side, 1, piece))

    def each_direct(act, count):
        def one(piece, carry):
            direct(piece, act)
            return carry
        lax.fori_loop(0, count, one, 0)

    each_detoured(lambda copy: copy.start())
    early = jnp.where(relays & at_end, pieces // 2, pieces)
    each_direct(lambda copy: copy.start(), early)

    def pass_on(index):
        for side in (0, 1):
            @pl.when(relays & leaves[side] & (index < detoured))
            def _(side=side):
                by_mirror(side, 0, index).wait_recv()
                by_mirror(side, 1, index).wait_recv()
                forward(side, index).start()

    def await_halo(piece):
        for side in (0, 1):
            turned = detours & enters[side] & (piece >= first)

            @pl.when(lands[side] & turned)
            def _(side=side):
                forward(side, piece - first).wait_recv()

            @pl.when(lands[side] & jnp.logical_not(turned))
            def _(side=side):
                halo(side, 0, piece).wait_recv()
                halo(side, 1, piece).wait_recv()

    @pl.when(jnp.logical_not(takes))
    def _():
        def start(tile, carry):
            for entry in range(8):
                arrived[tile, entry] = jnp.full((EIGHT, SPAN), (1.0, 0.0, 0.0, 1.0)[entry % 4], F32)
            return carry
        lax.fori_loop(0, tiles * units, start, 0)

    own_rows = rows + 2 * WMAX
    tall = own_rows + 2 * EIGHT * ninth

    def build(k, carry):
        half_width = width_ref[k]
        share = jnp.float32(1.0 / (2 * WMAX + 1) ** 2)
        for width in range(1, WMAX):
            share = jnp.where(half_width == width, jnp.float32(1.0 / (2 * width + 1) ** 2), share)
        nears[k] = near_ref[slot_ref[k]]
        strengths[k] = lens_ref[slot_ref[k]] * share
        place = lax.broadcasted_iota(jnp.int32, (rows, 2 * tall), 1)
        place = jnp.where(place >= tall, place - tall, place)
        far_up = jnp.where(place - own_rows == k, -WMAX - 1, FAR)
        far_down = jnp.where(place - own_rows - EIGHT * ninth == k, rows + WMAX, FAR)
        row = jnp.where(place < rows, place, jnp.where(
            place < rows + WMAX, place - rows - WMAX, jnp.where(
                place < own_rows, place - WMAX, jnp.where(
                    place < own_rows + EIGHT * ninth, far_up, far_down))))
        distance = row - lax.broadcasted_iota(jnp.int32, (rows, 2 * tall), 0)
        after, here, before = (inside(distance + shift, half_width) for shift in (-1, 0, 1))
        rowm[k, 0:rows, :] = here.astype(BF16)
        rowm[k, rows:2 * rows, :] = (after - before).astype(BF16)
        rowm[k, 2 * rows:3 * rows, :] = (after - 2.0 * here + before).astype(BF16)
        shape = (2 * LANES, LANES)
        gap = lax.broadcasted_iota(jnp.int32, shape, 0) - lax.broadcasted_iota(jnp.int32, shape, 1)
        colm[k] = inside(gap - LANES // 2, half_width).astype(BF16)
        return carry

    for copy in tables:
        copy.wait()
    lax.fori_loop(0, planes, build, 0)
    for copy in loads[1:]:
        copy.wait()

    def along_rows(chunk, k):
        window = pl.ds(pl.multiple_of(chunk * TILE, TILE), TILE)
        values = [own[k, :, window], top[k, :, window], bot[k, :, window]]
        values += [buffer[planes + i, :, window] for buffer in (top, bot) for i in range(ninth)]
        terms = jnp.concatenate(split(jnp.concatenate(values, axis=0)), axis=0)
        along[k, :, window] = jnp.dot(rowm[k], terms, preferred_element_type=F32)

    def along_columns(tile, k):
        col = pl.multiple_of(tile * TILE, TILE)
        lane = lax.broadcasted_iota(jnp.int32, (rows, LANES), 1)

        half_width, near, strength = width_ref[k], nears[k], strengths[k]

        def blocks(kind):
            return [along[k, kind * rows:(kind + 1) * rows, pl.ds(pl.multiple_of(col + i * LANES, LANES), LANES)]
                    for i in range(4)]

        def spread(values):
            turned = [pltpu.roll(value, LANES - half_width, 1) for value in values[1:]]
            ahead = [jnp.where(lane < LANES - half_width, turned[i], turned[i + 1]) for i in range(2)]
            turned = [pltpu.roll(value, half_width + 1, 1) for value in values[:-1]]
            behind = [jnp.where(lane > half_width, turned[i + 1], turned[i]) for i in range(2)]
            return jnp.concatenate([ahead[i] - behind[i] for i in range(2)], axis=1)

        def neighbours(values):
            turned = [pltpu.roll(value, LANES - 1, 1) for value in values]
            return [jnp.where(lane < LANES - 1, turned[i], turned[i + 1]) for i in range(3)] + turned[3:]

        boxed = blocks(0)
        xx = spread([after - here for after, here in zip(neighbours(boxed), boxed)])
        coef[k, 0, :, pl.ds(col, TILE)] = near - strength * xx
        slopes = blocks(1)
        xy = spread([after + here for after, here in zip(neighbours(slopes), slopes)])
        coef[k, 2, :, pl.ds(col, TILE)] = (-0.25 * strength) * xy
        turned = [pltpu.roll(value, LANES // 2, 1) for value in blocks(2)]
        halves = [jnp.where(lane < LANES // 2, turned[i], turned[i + 1]) for i in range(3)]
        terms = [split(half) for half in halves]
        stacked = jnp.concatenate([
            jnp.concatenate([terms[i][term], terms[i + 1][term]], axis=1)
            for i in range(2) for term in range(2)], axis=0)
        both = jnp.dot(stacked, colm[k], preferred_element_type=F32)
        yy = jnp.concatenate([
            both[2 * i * rows:(2 * i + 1) * rows] + both[(2 * i + 1) * rows:(2 * i + 2) * rows]
            for i in range(2)], axis=1)
        coef[k, 1, :, pl.ds(col, TILE)] = near - strength * yy

    def state(index):
        return pltpu.make_async_remote_copy(
            src_ref=leaving.at[index], dst_ref=arrived.at[index],
            send_sem=state_send.at[index], recv_sem=state_recv.at[index],
            device_id={"depth": depth + 1}, device_id_type=MESH,
        )

    def advance(tile, band):
        for part in range(parts):
            index = tile * units + band * parts + part
            band_rows = pl.ds(pl.multiple_of(band * EIGHT, EIGHT), EIGHT)
            lanes = pl.ds(pl.multiple_of(tile * TILE + part * SPAN, SPAN), SPAN)

            @pl.when(takes)
            def _(index=index):
                state(index).wait_recv()

            now = [arrived[index, entry] for entry in range(4)]
            past = [arrived[index, 4 + entry] for entry in range(4)]
            for k in range(planes):
                retained = 1.0 - nears[k]
                xx = coef[k, 0, band_rows, lanes]
                yy = coef[k, 1, band_rows, lanes]
                xy = coef[k, 2, band_rows, lanes]
                ahead = [
                    xx * now[0] + xy * now[2] + retained * past[0],
                    xx * now[1] + xy * now[3] + retained * past[1],
                    xy * now[0] + yy * now[2] + retained * past[2],
                    xy * now[1] + yy * now[3] + retained * past[3],
                ]
                now, past = ahead, now
                out_ref[k, band_rows, lanes] = 1.0 - 0.5 * (ahead[0] + ahead[3])
            for entry in range(4):
                leaving[index, entry] = now[entry]
                leaving[index, 4 + entry] = past[entry]

            @pl.when(gives)
            def _(index=index):
                state(index).start()

    await_halo(0)

    def rows_first(k, carry):
        along_rows(0, k)
        return carry

    lax.fori_loop(0, planes, rows_first, 0, unroll=4)
    def finish_halos():
        each_detoured(lambda copy: copy.wait_send())
        each_direct(lambda copy: copy.wait_send(), pieces)

        @pl.when(relays & outside)
        def _():
            def finish(index, carry):
                forward(0, index).wait_send()
                return carry
            lax.fori_loop(0, detoured, finish, 0)

    lead = jnp.clip(depth - (depth > 3).astype(jnp.int32), 1, tiles)

    def step(turn, carry):
        builds, moves = turn < tiles, turn >= lead

        @pl.when(builds)
        def _():
            await_halo(2 * turn + 1)

            @pl.when(turn < tiles - 1)
            def _():
                await_halo(2 * turn + 2)

        @pl.when(turn == tiles + lead - 1)
        def _():
            finish_halos()

        def share(band, carry):
            @pl.when(moves)
            def _():
                advance(turn - lead, band)

            @pl.when(builds)
            def _():
                group = range(planes // bands)
                for i in group:
                    along_rows(turn + 1, band * len(group) + i)
                for i in group:
                    along_columns(turn, band * len(group) + i)

            return carry

        lax.fori_loop(0, bands, share, 0)

        @pl.when(builds)
        def _():
            pass_on(2 * turn)
            pass_on(2 * turn + 1)
            for later in (early + 2 * turn, early + 2 * turn + 1):
                @pl.when(later < pieces)
                def _(later=later):
                    direct(later, lambda copy: copy.start())

        return carry

    lax.fori_loop(0, tiles + lead, step, 0)

    @pl.when(gives)
    def _():
        def finish(index, carry):
            state(index).wait_send()
            return carry
        lax.fori_loop(0, tiles * units, finish, 0)


def per_device(potential, widths, plane_slot, ratio_near, ratio_lens):
    planes, rows, cols = potential.shape
    ninth = round_up(planes, EIGHT) // EIGHT
    wide = cols + 2 * LANES
    tall = rows + 2 * WMAX + 2 * EIGHT * ninth
    states = (cols // SPAN) * (rows // EIGHT)
    table = ratio_near.shape[0]
    return pl.pallas_call(
        kernel,
        out_shape=pltpu.VMEM(potential.shape, F32),
        in_specs=[pl.BlockSpec(memory_space=pl.ANY)] * 5,
        out_specs=pl.BlockSpec(memory_space=pltpu.VMEM),
        scratch_shapes=[
            pltpu.SMEM((planes,), jnp.int32),
            pltpu.SMEM((planes,), jnp.int32),
            pltpu.SMEM((table,), F32),
            pltpu.SMEM((table,), F32),
            pltpu.VMEM((planes, rows, wide), F32),
            pltpu.VMEM((planes + ninth, EIGHT, wide), F32),
            pltpu.VMEM((planes + ninth, EIGHT, wide), F32),
            pltpu.VMEM((2, ninth, EIGHT, cols), F32),
            pltpu.VMEM((max(1, cols // LANES * DETOUR[0] // 16), planes + ninth, EIGHT, LANES), F32),
            pltpu.SMEM((planes,), F32),
            pltpu.SMEM((planes,), F32),
            pltpu.VMEM((planes, 3 * rows, 2 * tall), BF16),
            pltpu.VMEM((planes, 2 * LANES, LANES), BF16),
            pltpu.VMEM((planes, 3 * rows, wide), F32),
            pltpu.VMEM((planes, 3, rows, cols), F32),
            pltpu.VMEM((states, 8, EIGHT, SPAN), F32),
            pltpu.VMEM((states, 8, EIGHT, SPAN), F32),
            pltpu.SemaphoreType.DMA((3,)),
            pltpu.SemaphoreType.DMA((4,)),
            pltpu.SemaphoreType.DMA((2, 2, cols // LANES)),
            pltpu.SemaphoreType.DMA((2, 2, cols // LANES)),
            pltpu.SemaphoreType.DMA((2, max(1, cols // LANES * DETOUR[0] // 16))),
            pltpu.SemaphoreType.DMA((2, max(1, cols // LANES * DETOUR[0] // 16))),
            pltpu.SemaphoreType.DMA((max(1, cols // LANES * DETOUR[0] // 16),)),
            pltpu.SemaphoreType.DMA((states,)),
            pltpu.SemaphoreType.DMA((states,)),
        ],
        compiler_params=pltpu.CompilerParams(
            collective_id=0, has_side_effects=True, vmem_limit_bytes=48 * 2**20),
        name="lensing",
    )(*(pltpu.with_memory_space_constraint(table, pltpu.HBM) for table in (widths, plane_slot, ratio_near, ratio_lens)), potential)


def solution(mesh):
    return jax.shard_map(
        per_device,
        mesh=mesh,
        in_specs=(P("depth", "sky", None), P("depth"), P("depth"), P(), P()),
        out_specs=P("depth", "sky", None),
        check_vma=False,
    )
```

```python
import jax
import jax.numpy as jnp
from jax import lax
from jax.experimental import pallas as pl
from jax.experimental.pallas import tpu as pltpu
from jax.sharding import PartitionSpec as P

WMAX = 8
LANES = 128
EIGHT = 8
TILE = 256
SPAN = 128
FAR = 1000
PAIR = 2
DETOUR = (6, 3)
MESH = pl.DeviceIdType.MESH
F32 = jnp.float32
BF16 = jnp.bfloat16


def round_up(value, step):
    return -(-value // step) * step


def split(values):
    high = values.astype(BF16)
    return high, (values - high.astype(F32)).astype(BF16)


def inside(distance, half_width):
    return jnp.where(jnp.abs(distance) <= half_width, 1.0, 0.0)


def kernel(
    width_hbm, slot_hbm, near_hbm, lens_hbm, pot_ref, out_ref,
    width_ref, slot_ref, near_ref, lens_ref, own, top, bot, pack, relay, nears, strengths, rowm, colm, along, coef, arrived, leaving,
    load_sem, table_sem, halo_send, halo_recv, relay_send, relay_recv, forward_send, state_send, state_recv,
):
    depth, sky = lax.axis_index("depth"), lax.axis_index("sky")
    has_before, has_after = sky > 0, sky < lax.axis_size("sky") - 1
    takes, gives = depth > 0, depth < lax.axis_size("depth") - 1
    planes, rows, cols = pot_ref.shape
    ninth = pack.shape[1]
    pieces, tiles, parts = cols // LANES, cols // TILE, TILE // SPAN
    bands = rows // EIGHT
    units = parts * bands
    middle = pl.ds(LANES, cols)

    edges = ((WMAX, rows - 2 * WMAX), (0, WMAX), (rows - WMAX, WMAX))
    loads = [
        pltpu.make_async_copy(pot_ref.at[:, pl.ds(*part), :], own.at[:, pl.ds(*part), middle], load_sem.at[i])
        for i, part in enumerate(edges)]
    tables = [
        pltpu.make_async_copy(*pair, table_sem.at[i]) for i, pair in enumerate((
            (width_hbm, width_ref), (slot_hbm, slot_ref), (near_hbm, near_ref), (lens_hbm, lens_ref)))]
    for copy in loads + tables:
        copy.start()
    x, x_size = depth // PAIR, lax.axis_size("depth") // PAIR
    mirror = depth + PAIR * (x_size - 1 - 2 * x)
    detours, relays = x < x_size // 2, x >= x_size - x_size // 2
    at_end = (x == 0) | (x == x_size - 1)
    detoured = jnp.where(at_end, pieces * DETOUR[0] // 16, pieces * DETOUR[1] // 16)
    first = pieces - detoured
    odd = sky % 2 == 1
    leaves = (odd & has_after, jnp.logical_not(odd) & has_before)
    enters = (jnp.logical_not(odd) & has_before, odd & has_after)
    outside = leaves[0] | leaves[1]

    barrier = pltpu.get_barrier_semaphore()
    partners = (
        ((detours | relays) & outside, {"depth": mirror}),
        ((detours | relays) & leaves[0], {"depth": mirror, "sky": sky + 1}),
        ((detours | relays) & leaves[1], {"depth": mirror, "sky": sky - 1}),
        (has_before, {"sky": sky - 1}), (has_after, {"sky": sky + 1}),
        (takes, {"depth": depth - 1}), (gives, {"depth": depth + 1}),
    )
    for there, partner in partners:
        @pl.when(there)
        def _(partner=partner):
            pl.semaphore_signal(barrier, inc=1, device_id=partner, device_id_type=MESH)

    for buffer in (own, top, bot):
        for edge in (pl.ds(0, LANES), pl.ds(LANES + cols, LANES)):
            buffer[:, :, edge] = jnp.zeros((buffer.shape[0], buffer.shape[1], LANES), F32)
    for there, buffer in ((has_before, top), (has_after, bot)):
        @pl.when(jnp.logical_not(there))
        def _(buffer=buffer):
            buffer[...] = jnp.zeros_like(buffer)
    pack[...] = jnp.zeros_like(pack)
    loads[0].wait()
    for side, row in ((0, rows - WMAX - 1), (1, WMAX)):
        for k in range(planes):
            pack[side, k // EIGHT, pl.ds(k % EIGHT, 1), :] = own[k, pl.ds(row, 1), middle]

    pl.semaphore_wait(barrier, sum(there.astype(jnp.int32) for there, _ in partners))

    def halo(side, part, piece):
        col = pl.multiple_of(piece * LANES, LANES)
        landing = (top, bot)[side]
        lanes_there = pl.ds(pl.multiple_of(col + LANES, LANES), LANES)
        if part == 0:
            source = pot_ref.at[:, pl.ds((rows - WMAX, 0)[side], WMAX), pl.ds(col, LANES)]
            target = landing.at[pl.ds(0, planes), :, lanes_there]
        else:
            source = pack.at[side, :, :, pl.ds(col, LANES)]
            target = landing.at[pl.ds(planes, ninth), :, lanes_there]
        return pltpu.make_async_remote_copy(
            src_ref=source, dst_ref=target,
            send_sem=halo_send.at[side, part, piece], recv_sem=halo_recv.at[side, part, piece],
            device_id={"sky": sky + (1, -1)[side]}, device_id_type=MESH,
        )

    sends, lands = (has_after, has_before), (has_before, has_after)

    def by_mirror(side, part, index):
        col = pl.multiple_of((first + index) * LANES, LANES)
        if part == 0:
            source = pot_ref.at[:, pl.ds((rows - WMAX, 0)[side], WMAX), pl.ds(col, LANES)]
            target = relay.at[index, pl.ds(0, planes)]
        else:
            source = pack.at[side, :, :, pl.ds(col, LANES)]
            target = relay.at[index, pl.ds(planes, ninth)]
        return pltpu.make_async_remote_copy(
            src_ref=source, dst_ref=target,
            send_sem=relay_send.at[part, index], recv_sem=relay_recv.at[part, index],
            device_id={"depth": mirror}, device_id_type=MESH,
        )

    def forward(side, index):
        piece = first + index
        lanes_there = pl.ds(pl.multiple_of(piece * LANES + LANES, LANES), LANES)
        return pltpu.make_async_remote_copy(
            src_ref=relay.at[index], dst_ref=(top, bot)[side].at[:, :, lanes_there],
            send_sem=forward_send.at[index], recv_sem=halo_recv.at[side, 0, piece],
            device_id={"depth": mirror, "sky": sky + (1, -1)[side]}, device_id_type=MESH,
        )

    def each_detoured(act):
        for side in (0, 1):
            @pl.when(detours & leaves[side])
            def _(side=side):
                def one(index, carry):
                    act(by_mirror(side, 0, index))
                    act(by_mirror(side, 1, index))
                    return carry
                lax.fori_loop(0, detoured, one, 0)

    def direct(piece, act):
        for side in (0, 1):
            @pl.when(sends[side] & jnp.logical_not(detours & leaves[side] & (piece >= first)))
            def _(side=side):
                act(halo(side, 0, piece))
                act(halo(side, 1, piece))

    def each_direct(act, count):
        def one(piece, carry):
            direct(piece, act)
            return carry
        lax.fori_loop(0, count, one, 0)

    each_detoured(lambda copy: copy.start())
    early = jnp.where(relays & at_end, pieces // 2, pieces)
    each_direct(lambda copy: copy.start(), early)

    def pass_on(index):
        for side in (0, 1):
            @pl.when(relays & leaves[side] & (index < detoured))
            def _(side=side):
                by_mirror(side, 0, index).wait_recv()
                by_mirror(side, 1, index).wait_recv()
                forward(side, index).start()

    def await_halo(piece):
        for side in (0, 1):
            turned = detours & enters[side] & (piece >= first)

            @pl.when(lands[side] & turned)
            def _(side=side):
                forward(side, piece - first).wait_recv()

            @pl.when(lands[side] & jnp.logical_not(turned))
            def _(side=side):
                halo(side, 0, piece).wait_recv()
                halo(side, 1, piece).wait_recv()

    @pl.when(jnp.logical_not(takes))
    def _():
        def start(tile, carry):
            for entry in range(8):
                arrived[tile, entry] = jnp.full((EIGHT, SPAN), (1.0, 0.0, 0.0, 1.0)[entry % 4], F32)
            return carry
        lax.fori_loop(0, tiles * units, start, 0)

    own_rows = rows + 2 * WMAX
    tall = own_rows + 2 * EIGHT * ninth

    def build(k, carry):
        half_width = width_ref[k]
        share = jnp.float32(1.0 / (2 * WMAX + 1) ** 2)
        for width in range(1, WMAX):
            share = jnp.where(half_width == width, jnp.float32(1.0 / (2 * width + 1) ** 2), share)
        nears[k] = near_ref[slot_ref[k]]
        strengths[k] = lens_ref[slot_ref[k]] * share
        place = lax.broadcasted_iota(jnp.int32, (rows, 2 * tall), 1)
        place = jnp.where(place >= tall, place - tall, place)
        far_up = jnp.where(place - own_rows == k, -WMAX - 1, FAR)
        far_down = jnp.where(place - own_rows - EIGHT * ninth == k, rows + WMAX, FAR)
        row = jnp.where(place < rows, place, jnp.where(
            place < rows + WMAX, place - rows - WMAX, jnp.where(
                place < own_rows, place - WMAX, jnp.where(
                    place < own_rows + EIGHT * ninth, far_up, far_down))))
        distance = row - lax.broadcasted_iota(jnp.int32, (rows, 2 * tall), 0)
        after, here, before = (inside(distance + shift, half_width) for shift in (-1, 0, 1))
        rowm[k, 0:rows, :] = here.astype(BF16)
        rowm[k, rows:2 * rows, :] = (after - before).astype(BF16)
        rowm[k, 2 * rows:3 * rows, :] = (after - 2.0 * here + before).astype(BF16)
        shape = (2 * LANES, LANES)
        gap = lax.broadcasted_iota(jnp.int32, shape, 0) - lax.broadcasted_iota(jnp.int32, shape, 1)
        colm[k] = inside(gap - LANES // 2, half_width).astype(BF16)
        return carry

    for copy in tables:
        copy.wait()
    lax.fori_loop(0, planes, build, 0)
    for copy in loads[1:]:
        copy.wait()

    def along_rows(chunk, k):
        window = pl.ds(pl.multiple_of(chunk * TILE, TILE), TILE)
        values = [own[k, :, window], top[k, :, window], bot[k, :, window]]
        values += [buffer[planes + i, :, window] for buffer in (top, bot) for i in range(ninth)]
        terms = jnp.concatenate(split(jnp.concatenate(values, axis=0)), axis=0)
        along[k, :, window] = jnp.dot(rowm[k], terms, preferred_element_type=F32)

    def along_columns(tile, k):
        col = pl.multiple_of(tile * TILE, TILE)
        lane = lax.broadcasted_iota(jnp.int32, (rows, LANES), 1)

        half_width, near, strength = width_ref[k], nears[k], strengths[k]

        def blocks(kind):
            return [along[k, kind * rows:(kind + 1) * rows, pl.ds(pl.multiple_of(col + i * LANES, LANES), LANES)]
                    for i in range(4)]

        def spread(values):
            turned = [pltpu.roll(value, LANES - half_width, 1) for value in values[1:]]
            ahead = [jnp.where(lane < LANES - half_width, turned[i], turned[i + 1]) for i in range(2)]
            turned = [pltpu.roll(value, half_width + 1, 1) for value in values[:-1]]
            behind = [jnp.where(lane > half_width, turned[i + 1], turned[i]) for i in range(2)]
            return jnp.concatenate([ahead[i] - behind[i] for i in range(2)], axis=1)

        def neighbours(values):
            turned = [pltpu.roll(value, LANES - 1, 1) for value in values]
            return [jnp.where(lane < LANES - 1, turned[i], turned[i + 1]) for i in range(3)] + turned[3:]

        boxed = blocks(0)
        xx = spread([after - here for after, here in zip(neighbours(boxed), boxed)])
        coef[k, 0, :, pl.ds(col, TILE)] = near - strength * xx
        slopes = blocks(1)
        xy = spread([after + here for after, here in zip(neighbours(slopes), slopes)])
        coef[k, 2, :, pl.ds(col, TILE)] = (-0.25 * strength) * xy
        turned = [pltpu.roll(value, LANES // 2, 1) for value in blocks(2)]
        halves = [jnp.where(lane < LANES // 2, turned[i], turned[i + 1]) for i in range(3)]
        terms = [split(half) for half in halves]
        stacked = jnp.concatenate([
            jnp.concatenate([terms[i][term], terms[i + 1][term]], axis=1)
            for i in range(2) for term in range(2)], axis=0)
        both = jnp.dot(stacked, colm[k], preferred_element_type=F32)
        yy = jnp.concatenate([
            both[2 * i * rows:(2 * i + 1) * rows] + both[(2 * i + 1) * rows:(2 * i + 2) * rows]
            for i in range(2)], axis=1)
        coef[k, 1, :, pl.ds(col, TILE)] = near - strength * yy

    def state(index):
        return pltpu.make_async_remote_copy(
            src_ref=leaving.at[index], dst_ref=arrived.at[index],
            send_sem=state_send.at[index], recv_sem=state_recv.at[index],
            device_id={"depth": depth + 1}, device_id_type=MESH,
        )

    def advance(tile, band):
        for part in range(parts):
            index = tile * units + band * parts + part
            band_rows = pl.ds(pl.multiple_of(band * EIGHT, EIGHT), EIGHT)
            lanes = pl.ds(pl.multiple_of(tile * TILE + part * SPAN, SPAN), SPAN)

            @pl.when(takes)
            def _(index=index):
                state(index).wait_recv()

            now = [arrived[index, entry] for entry in range(4)]
            past = [arrived[index, 4 + entry] for entry in range(4)]
            for k in range(planes):
                retained = 1.0 - nears[k]
                xx = coef[k, 0, band_rows, lanes]
                yy = coef[k, 1, band_rows, lanes]
                xy = coef[k, 2, band_rows, lanes]
                ahead = [
                    xx * now[0] + xy * now[2] + retained * past[0],
                    xx * now[1] + xy * now[3] + retained * past[1],
                    xy * now[0] + yy * now[2] + retained * past[2],
                    xy * now[1] + yy * now[3] + retained * past[3],
                ]
                now, past = ahead, now
                out_ref[k, band_rows, lanes] = 1.0 - 0.5 * (ahead[0] + ahead[3])
            for entry in range(4):
                leaving[index, entry] = now[entry]
                leaving[index, 4 + entry] = past[entry]

            @pl.when(gives)
            def _(index=index):
                state(index).start()

    await_halo(0)

    def rows_first(k, carry):
        along_rows(0, k)
        return carry

    lax.fori_loop(0, planes, rows_first, 0, unroll=4)
    def finish_halos():
        each_detoured(lambda copy: copy.wait_send())
        each_direct(lambda copy: copy.wait_send(), pieces)

        @pl.when(relays & outside)
        def _():
            def finish(index, carry):
                forward(0, index).wait_send()
                return carry
            lax.fori_loop(0, detoured, finish, 0)

    lead = jnp.clip(depth - (depth > 3).astype(jnp.int32) - (depth > 5).astype(jnp.int32), 1, tiles)

    def step(turn, carry):
        builds, moves = turn < tiles, turn >= lead

        @pl.when(builds)
        def _():
            await_halo(2 * turn + 1)

            @pl.when(turn < tiles - 1)
            def _():
                await_halo(2 * turn + 2)

        @pl.when(turn == tiles + lead - 1)
        def _():
            finish_halos()

        def share(band, carry):
            @pl.when(moves)
            def _():
                advance(turn - lead, band)

            @pl.when(builds)
            def _():
                group = range(planes // bands)
                for i in group:
                    along_rows(turn + 1, band * len(group) + i)
                for i in group:
                    along_columns(turn, band * len(group) + i)

            return carry

        lax.fori_loop(0, bands, share, 0)

        @pl.when(builds)
        def _():
            pass_on(2 * turn)
            pass_on(2 * turn + 1)
            for later in (early + 2 * turn, early + 2 * turn + 1):
                @pl.when(later < pieces)
                def _(later=later):
                    direct(later, lambda copy: copy.start())

        return carry

    lax.fori_loop(0, tiles + lead, step, 0)

    @pl.when(gives)
    def _():
        def finish(index, carry):
            state(index).wait_send()
            return carry
        lax.fori_loop(0, tiles * units, finish, 0)


def per_device(potential, widths, plane_slot, ratio_near, ratio_lens):
    planes, rows, cols = potential.shape
    ninth = round_up(planes, EIGHT) // EIGHT
    wide = cols + 2 * LANES
    tall = rows + 2 * WMAX + 2 * EIGHT * ninth
    states = (cols // SPAN) * (rows // EIGHT)
    table = ratio_near.shape[0]
    return pl.pallas_call(
        kernel,
        out_shape=pltpu.VMEM(potential.shape, F32),
        in_specs=[pl.BlockSpec(memory_space=pl.ANY)] * 5,
        out_specs=pl.BlockSpec(memory_space=pltpu.VMEM),
        scratch_shapes=[
            pltpu.SMEM((planes,), jnp.int32),
            pltpu.SMEM((planes,), jnp.int32),
            pltpu.SMEM((table,), F32),
            pltpu.SMEM((table,), F32),
            pltpu.VMEM((planes, rows, wide), F32),
            pltpu.VMEM((planes + ninth, EIGHT, wide), F32),
            pltpu.VMEM((planes + ninth, EIGHT, wide), F32),
            pltpu.VMEM((2, ninth, EIGHT, cols), F32),
            pltpu.VMEM((max(1, cols // LANES * DETOUR[0] // 16), planes + ninth, EIGHT, LANES), F32),
            pltpu.SMEM((planes,), F32),
            pltpu.SMEM((planes,), F32),
            pltpu.VMEM((planes, 3 * rows, 2 * tall), BF16),
            pltpu.VMEM((planes, 2 * LANES, LANES), BF16),
            pltpu.VMEM((planes, 3 * rows, wide), F32),
            pltpu.VMEM((planes, 3, rows, cols), F32),
            pltpu.VMEM((states, 8, EIGHT, SPAN), F32),
            pltpu.VMEM((states, 8, EIGHT, SPAN), F32),
            pltpu.SemaphoreType.DMA((3,)),
            pltpu.SemaphoreType.DMA((4,)),
            pltpu.SemaphoreType.DMA((2, 2, cols // LANES)),
            pltpu.SemaphoreType.DMA((2, 2, cols // LANES)),
            pltpu.SemaphoreType.DMA((2, max(1, cols // LANES * DETOUR[0] // 16))),
            pltpu.SemaphoreType.DMA((2, max(1, cols // LANES * DETOUR[0] // 16))),
            pltpu.SemaphoreType.DMA((max(1, cols // LANES * DETOUR[0] // 16),)),
            pltpu.SemaphoreType.DMA((states,)),
            pltpu.SemaphoreType.DMA((states,)),
        ],
        compiler_params=pltpu.CompilerParams(
            collective_id=0, has_side_effects=True, vmem_limit_bytes=48 * 2**20),
        name="lensing",
    )(*(pltpu.with_memory_space_constraint(table, pltpu.HBM) for table in (widths, plane_slot, ratio_near, ratio_lens)), potential)


def solution(mesh):
    return jax.shard_map(
        per_device,
        mesh=mesh,
        in_specs=(P("depth", "sky", None), P("depth"), P("depth"), P(), P()),
        out_specs=P("depth", "sky", None),
        check_vma=False,
    )
```
